512 devices in a mesh: ctx: 64 (over z, y_hi, x), tp: 8 (over y_lo, core).
Axes of the slice: x: 4, y: 8 (y_hi: 2, y_lo: 4; y = y_hi * 4 + y_lo), z: 8, core: 2. Of those that a mesh axis runs over, the one named last changes fastest.
Arguments:
- tokens: bfloat16 [8192, 4096], P('ctx'), may hold values from -6 to 6
- weights: bfloat16 [8, 512, 3, 4096], P('tp', 'ctx'), may hold values from -0.09375 to 0.09375
- residues: float32 [8, 512, 16], P('tp', 'ctx'), may hold values from -1.5 to 1.5
- decay_rates: float32 [8, 512, 16], P('tp', 'ctx'), may hold values from 6.1035156e-05 to 0.03
- cotangent: bfloat16 [4096, 8192], P('tp', 'ctx'), may hold values from -6 to 6
Outputs:
- hyena_out: bfloat16 [4096, 8192], P('tp', 'ctx')
- grad_input: bfloat16 [8192, 4096], P('ctx', 'tp')
- grad_residue: float32 [8, 512, 16], P('tp', 'ctx')
The draws below stay inside these ranges and needn't reach their ends.
All inputs are finite; a program needn't handle non-finite values.
Results may differ from the reference program's by a relative error of at most 0.018.
Values may be sent and summed in bfloat16 or wider, within the bound.
A program may use at most 64 MiB of HBM per device.

```python
import math
import jax
import jax.numpy as jnp
from jax import lax

D = 4096
C = 4096
M = 16
L = 8192
C_TP = 512
N_TP = 8


def levels(key, extent, shards, low, top_value):
    level, own = 1.0, jax.random.fold_in(key, 6)
    for dim, parts in shards:
        draws = jnp.exp(jax.random.uniform(jax.random.fold_in(own, dim), (parts,), jnp.float32, low / len(shards), top_value / len(shards)))
        level = level * jnp.repeat(draws, extent[dim] // parts).reshape([-1 if axis == dim else 1 for axis in range(len(extent))])
    return level


def scatter_about(own_key, extent, width, reach, split=(), held_as=jnp.bfloat16):
    array = width * jax.random.normal(own_key, extent, jnp.float32)
    if split:
        array = array * levels(own_key, extent, split, -0.22, 0.18)
    return jnp.clip(array, -reach, reach).astype(held_as)


def setup_inputs(seed: int = 0) -> dict:
    key_list = jax.random.split(jax.random.key(seed), 6)
    return {
        "tokens": scatter_about(key_list[0], (L, D), 1.0, 6.0, ((0, 64),)),
        "weights": scatter_about(key_list[1], (N_TP, C_TP, 3, D), D ** -0.5, 0.09375, ((0, 8), (1, 64))),
        "residues": scatter_about(key_list[2], (N_TP, C_TP, M), 0.25, 1.5, ((0, 8), (1, 64)), jnp.float32),
        "decay_rates": jnp.clip(jnp.exp(math.log(0.03) - 6.1975026 * jax.random.uniform(key_list[3], (N_TP, C_TP, M), jnp.float32) ** levels(key_list[3], (N_TP, C_TP, M), ((0, 8), (1, 64)), -0.2, 0.2)), 6.103515625e-05, 0.03),
        "cotangent": scatter_about(key_list[4], (C, L), 1.0, 6.0, ((0, 8), (1, 64))),
    }


def reference(tokens, weights, residues, decay_rates, cotangent):
    flat_weights = weights.reshape(C, 3, D)
    projected = jnp.einsum('ld,cpd->cpl', tokens.astype(jnp.float32), flat_weights.astype(jnp.float32))
    features = projected.astype(jnp.bfloat16)
    query_f = features[:, 0].astype(jnp.float32)
    key_part = features[:, 1].astype(jnp.float32)
    value_part = features[:, 2].astype(jnp.float32)
    gated_in = (key_part * value_part).astype(jnp.bfloat16)
    rate_all = decay_rates.reshape(C, M)
    residue_all = residues.reshape(C, M)
    position = jnp.arange(L, dtype=jnp.float32)

    def mode_basis(mode_index):
        rate_col = rate_all[:, mode_index][:, None]
        return jnp.sqrt(2.0 * rate_col) * jnp.exp(-rate_col * position[None, :])
    taps_full = jnp.zeros((C, L), jnp.float32)
    for mode_index in range(M):
        taps_full = taps_full + residue_all[:, mode_index][:, None] * mode_basis(mode_index)
    padded = 2 * L
    gated_spec = jnp.fft.rfft(gated_in.astype(jnp.float32), n=padded, axis=1)
    taps_spec = jnp.fft.rfft(taps_full, n=padded, axis=1)
    conv_out = jnp.fft.irfft(gated_spec * taps_spec, n=padded, axis=1)[:, :L].astype(jnp.bfloat16)
    hyena_out = (query_f * conv_out.astype(jnp.float32)).astype(jnp.bfloat16)
    slope_in = (cotangent.astype(jnp.float32) * query_f).astype(jnp.bfloat16)
    slope_spec = jnp.fft.rfft(slope_in.astype(jnp.float32), n=padded, axis=1)
    back_in = jnp.fft.irfft(jnp.conj(taps_spec) * slope_spec, n=padded, axis=1)[:, :L].astype(jnp.bfloat16)
    taps_grad = jnp.fft.irfft(jnp.conj(gated_spec) * slope_spec, n=padded, axis=1)[:, :L]
    columns = [lax.optimization_barrier(jnp.sum(taps_grad * mode_basis(mode_index), axis=1)) for mode_index in range(M)]
    grad_residue = (jnp.stack(columns, axis=1) / jnp.sqrt(jnp.float32(L))).reshape(N_TP, C_TP, M)
    back_f = back_in.astype(jnp.float32)
    grad_query = (cotangent.astype(jnp.float32) * conv_out.astype(jnp.float32)).astype(jnp.bfloat16)
    grad_key = (back_f * value_part).astype(jnp.bfloat16)
    grad_value = (back_f * key_part).astype(jnp.bfloat16)
    grad_proj = jnp.stack([grad_query, grad_key, grad_value], axis=1)
    summed = jnp.zeros((L, D), jnp.float32)
    for block_index in range(N_TP):
        first = block_index * C_TP
        partial_value = jnp.einsum('cpl,cpd->ld', grad_proj[first:first + C_TP].astype(jnp.float32), flat_weights[first:first + C_TP].astype(jnp.float32))
        rounded = lax.optimization_barrier(partial_value.astype(jnp.bfloat16))
        summed = summed + rounded.astype(jnp.float32)
    grad_input = summed.astype(jnp.bfloat16)
    return (hyena_out, grad_input, grad_residue)
```

```python
import functools
import math

import jax
import jax.numpy as jnp
from jax import lax
from jax.experimental import pallas as pl
from jax.experimental.pallas import tpu as pltpu
from jax.sharding import Mesh, PartitionSpec as P

AXES = ("z", "h", "x", "l", "c")
SIZES = (8, 2, 4, 4, 2)
Z, H, X, NL, NC = SIZES
ZH = Z * H
MESH = pl.DeviceIdType.MESH
F32 = jnp.float32
BF16 = jnp.bfloat16

D = 4096
POS = 128
OWN = 8
CH = ZH * OWN
ROWS = X * POS
M = 16
SUB = 64
COLS = D // (NL * NC)
HALF = COLS // 2
UNIT = POS // 4
ORDER = (0, 3, 1, 2)
STEPS = ((Z // 2, Z - 1 - Z // 2), (Z - 1 - Z // 2, Z // 2))


def remote(src, dst, send, recv, device):
    return pltpu.make_async_remote_copy(
        src_ref=src, dst_ref=dst, send_sem=send, recv_sem=recv,
        device_id=device, device_id_type=MESH,
    )


def rounded(value):
    return value.astype(BF16).astype(F32)


def tree_sum(terms):
    terms = list(terms)
    while len(terms) > 1:
        terms = [
            terms[i] + terms[i + 1] if i + 1 < len(terms) else terms[i]
            for i in range(0, len(terms), 2)
        ]
    return terms[0]


def rows_of(index, count):
    return pl.ds(pl.multiple_of(index * count, count), count)


def body(
    length,
    tok, wts, res, rate, cot,
    hyena_out, grad_input, grad_residue,
    tk, wg, coef_own, coef, cotv,
    q_s, k_s, v_s, g_s, s_s, cot_s, conv_s, back_s,
    a_t, r_t, cl_t, cb_t, eb, pb, st, gr_s, gr_t, gr_r,
    hy_t, hy_o, g_mat, acc, d_s, d_r, m1_s, m1_r, m2_s, m2_r, y_s, y_r, y_own,
    loc_sem, w_ss, w_rs, c_ss, c_rs, h_ss, h_rs, t_ss, t_rs, p_ss, p_rs,
    ct_ss, ct_rs, pb_ss, pb_rs, st_ss, st_rs, gr_ss, gr_rs, hy_ss, hy_rs,
    d_ss, d_rs, m1_ss, m1_rs, m2_ss, m2_rs, y_ss, y_rs,
):
    z, h, x = lax.axis_index("z"), lax.axis_index("h"), lax.axis_index("x")
    ell, core = lax.axis_index("l"), lax.axis_index("c")
    me = z * H + h
    z_up, z_down = lax.rem(z + 1, Z), lax.rem(z + Z - 1, Z)
    x_up, x_down, x_far = lax.rem(x + 1, X), lax.rem(x + X - 1, X), lax.rem(x + 2, X)
    mate = me + 1 - 2 * h
    sends = []

    coef_own[...] = jnp.zeros_like(coef_own)
    coef_own[0, :, 0:M] = res[0]
    coef_own[1, :, 0:M] = rate[0]
    local = [
        pltpu.make_async_copy(tok, tk.at[rows_of(x, POS), :], loc_sem.at[0]),
        pltpu.make_async_copy(wts, wg.at[:, rows_of(me, OWN), :], loc_sem.at[1]),
        pltpu.make_async_copy(cot.at[:, x], cotv.at[x], loc_sem.at[2]),
    ]
    for copy in local:
        copy.start()
    coef[:, rows_of(me, OWN), :] = coef_own[...]

    barrier = pltpu.get_barrier_semaphore()
    peers = [{"z": z_up}, {"z": z_down}, {"h": 1 - h}, {"c": 1 - core}]
    peers += [{"x": lax.rem(x + i, X)} for i in range(1, X)]
    peers += [{"l": lax.rem(ell + i, NL)} for i in range(1, NL)]
    for peer in peers:
        pl.semaphore_signal(barrier, inc=1, device_id=peer, device_id_type=MESH)
    pl.semaphore_wait(barrier, len(peers))

    def ring(stream, way, step):
        from_z = lax.rem(z - step + Z, Z) if way == 0 else lax.rem(z + step, Z)
        block = from_z * H + (h if stream == 0 else 1 - h)
        slot = wg.at[:, rows_of(block, OWN), :]
        cslot = coef.at[:, rows_of(block, OWN), :]
        own = stream == 0 and step == 0
        to = {"z": z_up if way == 0 else z_down}
        return (
            remote(wts if own else slot, slot, w_ss.at[stream, way, step], w_rs.at[stream, way, step], to),
            remote(coef_own if own else cslot, cslot, c_ss.at[stream, way, step], c_rs.at[stream, way, step], to),
        )

    def launch(copies):
        for copy in copies:
            copy.start()
            sends.append(copy)
        return copies

    def arrived(copies):
        for copy in copies:
            copy.wait_recv()

    def unit(source, u):
        return tk.at[pl.ds(pl.multiple_of(source * POS + core * (POS // 2) + u * UNIT, UNIT), UNIT), :]

    def own_unit(u):
        return tok.at[pl.ds(pl.multiple_of(core * (POS // 2) + u * UNIT, UNIT), UNIT), :]

    def tok_own(way, u):
        to = {"x": x_up if way == 0 else x_down}
        return remote(own_unit(u), unit(x, u), t_ss.at[way, u], t_rs.at[way, u], to)

    def tok_far(way):
        to = {"x": x_up if way == 0 else x_down}
        src = unit(x_down if way == 0 else x_up, way)
        return remote(src, src, t_ss.at[way, 2], t_rs.at[way, 2], to)

    def pass_on(index, source, u):
        src = unit(source, u)
        return remote(src, src, p_ss.at[index], p_rs.at[index], {"c": 1 - core})

    mate_slot = wg.at[:, rows_of(me, OWN), :]
    to_mate = launch((
        remote(wts, mate_slot, h_ss.at[0], h_rs.at[0], {"h": 1 - h}),
        remote(coef_own, coef.at[:, rows_of(me, OWN), :], h_ss.at[1], h_rs.at[1], {"h": 1 - h}),
    ))
    flying = {}
    for way in (0, 1):
        flying[0, way] = launch(ring(0, way, 0))
    toks = {}
    for way, u in ((0, 0), (1, 1), (0, 1), (1, 0)):
        toks[way, u] = launch((tok_own(way, u),))
    cots = [
        remote(cot.at[:, lax.rem(x + i, X)], cotv.at[x], ct_ss.at[i - 1], ct_rs.at[i - 1], {"x": lax.rem(x + i, X)})
        for i in range(1, X)
    ]
    launch(cots)

    def advance(stream, step):
        for way in (0, 1):
            if step < STEPS[stream][way]:
                arrived(flying[stream, way])
                if step + 1 < STEPS[stream][way]:
                    flying[stream, way] = launch(ring(stream, way, step + 1))

    passes = []
    arrived(toks[0, 0])
    far_up = launch((tok_far(0),))
    passes += launch((pass_on(0, x_down, 0),))
    arrived(toks[1, 1])
    far_down = launch((tok_far(1),))
    passes += launch((pass_on(1, x_up, 1),))
    advance(0, 0)
    arrived(to_mate)
    for way in (0, 1):
        flying[1, way] = launch(ring(1, way, 0))
    arrived(toks[0, 1])
    passes += launch((pass_on(2, x_down, 1),))
    arrived(toks[1, 0])
    passes += launch((pass_on(3, x_up, 0),))
    advance(0, 1)
    advance(1, 0)
    arrived(far_up)
    passes += launch((pass_on(4, x_far, 0),))
    arrived(far_down)
    passes += launch((pass_on(5, x_far, 1),))
    advance(0, 2)
    advance(1, 1)
    arrived(cots)
    advance(0, 3)
    advance(1, 2)
    arrived(passes)
    advance(1, 3)
    for copy in local:
        copy.wait()

    def project(i, carry):
        out = lax.dot_general(
            tk[rows_of(i, POS), :], wg[...].reshape(3 * CH, D),
            (((1,), (1,)), ((), ())), preferred_element_type=F32,
        )
        q_s[rows_of(i, POS), :] = rounded(out[:, 0:CH])
        k_s[rows_of(i, POS), :] = rounded(out[:, CH:2 * CH])
        v_s[rows_of(i, POS), :] = rounded(out[:, 2 * CH:3 * CH])
        return carry

    lax.fori_loop(0, X, project, 0)

    def gate(i, carry):
        at = rows_of(i, POS)
        cot_s[at, :] = jnp.transpose(cotv[i].astype(F32).reshape(CH, POS))
        g_s[at, :] = rounded(k_s[at, :] * v_s[at, :])
        s_s[at, :] = rounded(cot_s[at, :] * q_s[at, :])
        return carry

    lax.fori_loop(0, X, gate, 0)

    residue = jnp.transpose(coef[0])[0:M, :]
    decay = jnp.transpose(coef[1])[0:M, :]
    width = jnp.sqrt(2.0 * decay)
    once = jnp.exp(-decay)
    scaled = residue * width
    for m in range(M):
        a_t[m] = jnp.broadcast_to(once[m:m + 1, :], (8, CH))
        r_t[m] = jnp.broadcast_to(scaled[m:m + 1, :], (8, CH))

    def states(t, carry):
        up, down = carry
        g_now = g_s[pl.ds(t, 8, stride=SUB), :]
        s_now = s_s[pl.ds(SUB - 1 - t, 8, stride=SUB), :]
        return (
            tuple(a_t[m] * up[m] + g_now for m in range(M)),
            tuple(a_t[m] * down[m] + s_now for m in range(M)),
        )

    zero = tuple(jnp.zeros((8, CH), F32) for _ in range(M))
    up, down = lax.fori_loop(0, SUB, states, (zero, zero))
    piece = lax.broadcasted_iota(jnp.int32, (8, CH), 0)
    for m in range(M):
        lost = decay[m:m + 1, :]
        fore, aft = up[m], down[m]
        for shift in (1, 2, 4):
            keep = jnp.exp(lost * (-float(SUB * shift)))
            fore = fore + jnp.where(piece >= shift, keep * pltpu.roll(fore, shift, 0), 0.0)
            aft = aft + jnp.where(piece < 8 - shift, keep * pltpu.roll(aft, 8 - shift, 0), 0.0)
        eb[0, m:m + 1, :] = fore[7:8, :]
        eb[1, m:m + 1, :] = aft[0:1, :]
        cl_t[m] = jnp.where(piece >= 1, pltpu.roll(fore, 1, 0), 0.0)
        cb_t[m] = jnp.where(piece < 7, pltpu.roll(aft, 7, 0), 0.0)

    to_pair = launch((remote(eb, pb, pb_ss, pb_rs, {"h": 1 - h}),))
    direct = []
    for i in range(1, Z):
        to_z = lax.rem(z + i, Z)
        which = jnp.where(to_z > z, 0, 1)
        direct.append(remote(eb.at[which], st.at[me], st_ss.at[0, i], st_rs.at[0, i], {"z": to_z}))
    launch(direct)
    arrived(to_pair)
    relayed = []
    for i in range(1, Z):
        to_z = lax.rem(z + i, Z)
        which = jnp.where(to_z > z, 0, 1)
        relayed.append(remote(pb.at[which], st.at[mate], st_ss.at[1, i], st_rs.at[1, i], {"z": to_z}))
    launch(relayed)
    st[mate] = pb[1 - h]
    arrived(direct)
    arrived(relayed)

    far_keep = jnp.exp(decay * (-float(ROWS)))
    none = jnp.zeros((M, CH), F32)
    before = lax.fori_loop(0, me, lambda j, s: far_keep * s + st[j], none)
    after = lax.fori_loop(0, ZH - 1 - me, lambda j, s: far_keep * s + st[ZH - 1 - j], none)

    place = piece.astype(F32) * float(SUB)
    start_up, start_down = [], []
    for m in range(M):
        lost = decay[m:m + 1, :]
        start_up.append(cl_t[m] + jnp.exp(-lost * place) * before[m:m + 1, :])
        start_down.append(
            cb_t[m] + jnp.exp(-lost * (float(SUB * 7) - place)) * after[m:m + 1, :]
        )

    def forward(t, carry):
        up, total = carry
        at = pl.ds(t, 8, stride=SUB)
        g_now, s_now = g_s[at, :], s_s[at, :]
        up = tuple(a_t[m] * up[m] + g_now for m in range(M))
        conv_s[at, :] = tree_sum(r_t[m] * up[m] for m in range(M))
        return up, tuple(total[m] + s_now * up[m] for m in range(M))

    def backward(t, down):
        at = pl.ds(SUB - 1 - t, 8, stride=SUB)
        s_now = s_s[at, :]
        down = tuple(a_t[m] * down[m] + s_now for m in range(M))
        back_s[at, :] = tree_sum(r_t[m] * down[m] for m in range(M))
        return down

    _, total = lax.fori_loop(0, SUB, forward, (tuple(start_up), zero))
    lax.fori_loop(0, SUB, backward, tuple(start_down))

    def gates(i, carry):
        at = rows_of(i, POS)
        conv, back = rounded(conv_s[at, :]), rounded(back_s[at, :])
        g_mat[at, 0:CH] = (cot_s[at, :] * conv).astype(BF16)
        g_mat[at, CH:2 * CH] = (back * v_s[at, :]).astype(BF16)
        g_mat[at, 2 * CH:3 * CH] = (back * k_s[at, :]).astype(BF16)
        hyena = jnp.transpose(q_s[at, :] * conv)
        hy_t[i] = hyena.reshape(ZH, OWN, POS).astype(BF16)
        return carry

    lax.fori_loop(0, X, gates, 0)
    hyenas = [
        remote(hy_t.at[lax.rem(x + i, X)], hy_o.at[:, x], hy_ss.at[i - 1], hy_rs.at[i - 1], {"x": lax.rem(x + i, X)})
        for i in range(1, X)
    ]
    launch(hyenas)
    hy_o[:, x] = hy_t[x]

    gr_s[...] = jnp.zeros_like(gr_s)
    norm = 1.0 / math.sqrt(length)
    for m in range(M):
        gr_s[m:m + 1, :] = jnp.sum(total[m], axis=0, keepdims=True) * (width[m:m + 1, :] * norm)
    gr_t[...] = jnp.transpose(gr_s[...])
    owners = []
    for i in range(1, ZH):
        to = lax.rem(me + i, ZH)
        owners.append(remote(
            gr_t.at[rows_of(to, OWN), :], gr_r.at[i], gr_ss.at[i], gr_rs.at[i],
            {"z": lax.div(to, H), "h": lax.rem(to, H)},
        ))
    launch(owners)

    def product(j, mine):
        parity = core if mine else 1 - core
        col = pl.multiple_of((j * NC + parity) * COLS, COLS)

        def tile(i, carry):
            at = rows_of(i, 2 * POS)
            out = jnp.dot(
                g_mat[at, :], wg[:, :, pl.ds(col, COLS)].reshape(3 * CH, COLS),
                preferred_element_type=F32,
            )
            if mine:
                acc[j, at, :] = out
            else:
                d_s[j, at, :] = out.astype(BF16)
            return carry

        lax.fori_loop(0, ROWS // (2 * POS), tile, 0)

    def chip_sum(j, owner):
        at = rows_of(owner, POS)
        return acc[j, at, :] + d_r[j, at, :].astype(F32)

    cores, first, second, finals = {}, {}, {}, {}
    for j in ORDER:
        product(j, False)
        cores[j] = launch((remote(d_s.at[j], d_r.at[j], d_ss.at[j], d_rs.at[j], {"c": 1 - core}),))
        product(j, True)

    def stage_first(j):
        arrived(cores[j])
        far = chip_sum(j, x_far)
        m1_s[j, 0] = far[:, 0:HALF].astype(BF16)
        m1_s[j, 1] = far[:, HALF:COLS].astype(BF16)
        first[j] = launch([
            remote(m1_s.at[j, w], m1_r.at[j, w], m1_ss.at[j, w], m1_rs.at[j, w], {"x": x_up if w == 0 else x_down})
            for w in (0, 1)
        ])

    def stage_second(j):
        arrived(first[j])
        for w in (0, 1):
            near = chip_sum(j, x_up if w == 0 else x_down)
            cut = slice(0, HALF) if w == 0 else slice(HALF, COLS)
            rest = slice(HALF, COLS) if w == 0 else slice(0, HALF)
            m2_s[j, w, :, cut] = (near[:, cut] + m1_r[j, w].astype(F32)).astype(BF16)
            m2_s[j, w, :, rest] = near[:, rest].astype(BF16)
        second[j] = launch([
            remote(m2_s.at[j, w], m2_r.at[j, w], m2_ss.at[j, w], m2_rs.at[j, w], {"x": x_up if w == 0 else x_down})
            for w in (0, 1)
        ])

    def stage_third(j):
        arrived(second[j])
        total_x = chip_sum(j, x) + m2_r[j, 0].astype(F32) + m2_r[j, 1].astype(F32)
        copy = remote(y_s.at[j], y_r.at[ell], y_ss.at[j], y_rs.at[ell], {"l": jnp.int32(j)})
        finals[j] = copy

        @pl.when(ell == j)
        def _():
            y_own[...] = total_x

        @pl.when(ell != j)
        def _():
            y_s[j] = total_x.astype(BF16)
            copy.start()

    first_of, n = ORDER, len(ORDER)
    for i in range(n + 2):
        if i < n:
            stage_first(first_of[i])
        if 0 <= i - 1 < n:
            stage_second(first_of[i - 1])
        if 0 <= i - 2 < n:
            stage_third(first_of[i - 2])

    arrived(hyenas)
    hyena_out[...] = hy_o[...]
    arrived(owners)
    share = gr_t[rows_of(me, OWN), :]
    for i in range(1, ZH):
        share = share + gr_r[i]
    grad_residue[...] = share[:, 0:M]
    for j in range(NL):
        @pl.when(ell != j)
        def _():
            remote(y_s.at[j], y_r.at[j], y_ss.at[j], y_rs.at[j], {"l": jnp.int32(j)}).wait_recv()
            y_own[...] += y_r[j].astype(F32)
            finals[j].wait_send()
    grad_input[...] = y_own[...].astype(BF16)
    for copy in sends:
        copy.wait_send()


def shards(tokens, weights, residues, decay_rates, cotangent, length):
    wts = jnp.transpose(weights[0], (1, 0, 2))
    cot = cotangent.reshape(ZH, X, OWN, POS)
    dma = pltpu.SemaphoreType.DMA
    scratch = [
        pltpu.VMEM((ROWS, D), BF16),
        pltpu.VMEM((3, CH, D), BF16),
        pltpu.VMEM((2, OWN, 128), F32),
        pltpu.VMEM((2, CH, 128), F32),
        pltpu.VMEM((X, ZH, OWN, POS), BF16),
    ]
    scratch += [pltpu.VMEM((ROWS, CH), F32)] * 8
    scratch += [pltpu.VMEM((M, 8, CH), F32)] * 4
    scratch += [
        pltpu.VMEM((2, M, CH), F32),
        pltpu.VMEM((2, M, CH), F32),
        pltpu.VMEM((ZH, M, CH), F32),
        pltpu.VMEM((CH, CH), F32),
        pltpu.VMEM((CH, CH), F32),
        pltpu.VMEM((ZH, OWN, CH), F32),
        pltpu.VMEM((X, ZH, OWN, POS), BF16),
        pltpu.VMEM((ZH, X, OWN, POS), BF16),
        pltpu.VMEM((ROWS, 3 * CH), BF16),
        pltpu.VMEM((NL, ROWS, COLS), F32),
        pltpu.VMEM((NL, ROWS, COLS), BF16),
        pltpu.VMEM((NL, ROWS, COLS), BF16),
        pltpu.VMEM((NL, 2, POS, HALF), BF16),
        pltpu.VMEM((NL, 2, POS, HALF), BF16),
        pltpu.VMEM((NL, 2, POS, COLS), BF16),
        pltpu.VMEM((NL, 2, POS, COLS), BF16),
        pltpu.VMEM((NL, POS, COLS), BF16),
        pltpu.VMEM((NL, POS, COLS), BF16),
        pltpu.VMEM((POS, COLS), F32),
    ]
    steps = Z // 2
    scratch += [dma((3,))]
    for shape in (
        (2, 2, steps), (2, 2, steps), (2,), (2, 3), (6,), (X - 1,), (), (2, Z), (ZH,), (X - 1,),
        (NL,), (NL, 2), (NL, 2), (NL,),
    ):
        scratch += [dma(shape) if shape else dma, dma(shape) if shape else dma]
    vmem, hbm = pl.BlockSpec(memory_space=pltpu.VMEM), pl.BlockSpec(memory_space=pl.ANY)
    hyena, grad, residue = pl.pallas_call(
        functools.partial(body, length),
        out_shape=(
            jax.ShapeDtypeStruct((ZH, X, OWN, POS), BF16),
            jax.ShapeDtypeStruct((POS, COLS), BF16),
            jax.ShapeDtypeStruct((OWN, M), F32),
        ),
        in_specs=[hbm, hbm, vmem, vmem, hbm],
        out_specs=(vmem, vmem, vmem),
        scratch_shapes=scratch,
        compiler_params=pltpu.CompilerParams(
            collective_id=0, has_side_effects=True, vmem_limit_bytes=60 * 1024 * 1024
        ),
        name="hyena_block",
    )(tokens, wts, residues, decay_rates, cot)
    return (hyena.reshape(X * ZH * OWN, POS), grad, residue[None])


def solution(mesh):
    fine = Mesh(mesh.devices.reshape(SIZES), AXES)
    ctx, tp = ("z", "h", "x"), ("l", "c")

    def step(tokens, weights, residues, decay_rates, cotangent):
        return jax.shard_map(
            functools.partial(shards, length=tokens.shape[0]),
            mesh=fine,
            in_specs=(P(ctx, None), P(tp, ctx), P(tp, ctx), P(tp, ctx), P(tp, ctx)),
            out_specs=(P(tp, ctx), P(ctx, tp), P(tp, ctx)),
            check_vma=False,
        )(tokens, weights, residues, decay_rates, cotangent)

    return step
```

```python
import functools
import heapq
import math

import jax
import jax.numpy as jnp
from jax import lax
from jax.experimental import pallas as pl
from jax.experimental.pallas import tpu as pltpu
from jax.sharding import Mesh, PartitionSpec as P

AXES = ("z", "h", "x", "l", "c")
SIZES = (8, 2, 4, 4, 2)
Z, H, X, NL, NC = SIZES
ZH = Z * H
MESH = pl.DeviceIdType.MESH
F32 = jnp.float32
BF16 = jnp.bfloat16

D = 4096
POS = 128
OWN = 8
CH = ZH * OWN
ROWS = X * POS
M = 16
SUB = 64
COLS = D // (NL * NC)
PARTS = 2
WIDE = COLS // PARTS
HALF = WIDE // 2
PIECES = NL * PARTS
UNIT = POS // 4
CUT = D // 2
CHUNKS = 6
ORDER = (0, 6, 1, 7, 2, 4, 3, 5)
STEPS = ((Z // 2, Z - 1 - Z // 2), (Z - 1 - Z // 2, Z // 2))


def arrival_order():
    cost = {"z": 0.7, "h": 1.4, "x": 5.6, "c": 0.8}
    delay = {"z": 3.5, "h": 5.0, "x": 2.5, "c": 1.5}
    free, queue, order = {}, [], []

    def send(now, link, message):
        free[link] = max(now, free.get(link, 0.0)) + cost[link[0]]
        heapq.heappush(queue, (free[link] + delay[link[0]], len(order) + len(queue), message))

    for p in range(CHUNKS):
        for way in (0, 1):
            send(0.0, ("z", way), ("ring", 0, way, 0, p))
        send(0.0, ("h",), ("mate", p))
    for way in (0, 1):
        for u in (way, 1 - way):
            send(0.0, ("x", way), ("near", way, u))
    while queue:
        now, _, message = heapq.heappop(queue)
        order.append(message)
        if message[0] == "ring":
            _, stream, way, step, p = message
            if step + 1 < STEPS[stream][way]:
                send(now, ("z", way), ("ring", stream, way, step + 1, p))
        elif message[0] == "mate":
            for way in (0, 1):
                send(now, ("z", way), ("ring", 1, way, 0, message[1]))
        elif message[0] == "near":
            _, way, u = message
            if u == way:
                send(now, ("x", way), ("far", way))
            send(now, ("c",), ("pass", 2 * way + u))
        elif message[0] == "far":
            send(now, ("c",), ("pass", 4 + message[1]))
    return order


def remote(src, dst, send, recv, device):
    return pltpu.make_async_remote_copy(
        src_ref=src, dst_ref=dst, send_sem=send, recv_sem=recv,
        device_id=device, device_id_type=MESH,
    )


def rounded(value):
    return value.astype(BF16).astype(F32)


def tree_sum(terms):
    terms = list(terms)
    while len(terms) > 1:
        terms = [
            terms[i] + terms[i + 1] if i + 1 < len(terms) else terms[i]
            for i in range(0, len(terms), 2)
        ]
    return terms[0]


def rows_of(index, count):
    return pl.ds(pl.multiple_of(index * count, count), count)


def body(
    length,
    tok, wts, res, rate, cot,
    hyena_out, grad_input, grad_residue,
    tk, wg, coef_own, coef, cotv,
    q_s, k_s, v_s, g_s, s_s, cot_s, conv_s, back_s,
    a_t, r_t, cl_t, cb_t, eb, st, gr_s, gr_t, gr_r,
    hy_t, hy_o, g_mat, acc, d_s, d_r, m1_s, m1_r, m2_s, m2_r, y_s, y_r, y_own,
    loc_sem, w_ss, w_rs, c_ss, c_rs, h_ss, h_rs, t_ss, t_rs, p_ss, p_rs,
    ct_ss, ct_rs, st_ss, st_rs, gr_ss, gr_rs, hy_ss, hy_rs,
    d_ss, d_rs, m1_ss, m1_rs, m2_ss, m2_rs, y_ss, y_rs,
):
    z, h, x = lax.axis_index("z"), lax.axis_index("h"), lax.axis_index("x")
    ell, core = lax.axis_index("l"), lax.axis_index("c")
    me = z * H + h
    z_up, z_down = lax.rem(z + 1, Z), lax.rem(z + Z - 1, Z)
    x_up, x_down, x_far = lax.rem(x + 1, X), lax.rem(x + X - 1, X), lax.rem(x + 2, X)
    sends = []

    coef_own[...] = jnp.zeros_like(coef_own)
    coef_own[:, 0:M] = res[0]
    coef_own[:, M:2 * M] = rate[0]
    local = [
        pltpu.make_async_copy(tok, tk.at[rows_of(x, POS), :], loc_sem.at[0]),
        pltpu.make_async_copy(wts, wg.at[:, rows_of(me, OWN), :], loc_sem.at[1]),
        pltpu.make_async_copy(cot.at[:, x], cotv.at[x], loc_sem.at[2]),
    ]
    for copy in local:
        copy.start()
    coef[rows_of(me, OWN), :] = coef_own[...]

    barrier = pltpu.get_barrier_semaphore()
    peers = [{"z": z_up}, {"z": z_down}, {"h": 1 - h}, {"c": 1 - core}]
    peers += [{"x": lax.rem(x + i, X)} for i in range(1, X)]
    peers += [{"l": lax.rem(ell + i, NL)} for i in range(1, NL)]
    for peer in peers:
        pl.semaphore_signal(barrier, inc=1, device_id=peer, device_id_type=MESH)
    pl.semaphore_wait(barrier, len(peers))

    def launch(copies):
        for copy in copies:
            copy.start()
            sends.append(copy)
        return copies

    def arrived(copies):
        for copy in copies:
            copy.wait_recv()

    def ring(stream, way, step, p):
        from_z = lax.rem(z - step + Z, Z) if way == 0 else lax.rem(z + step, Z)
        block = from_z * H + (h if stream == 0 else 1 - h)
        cut = pl.ds(p % 2 * CUT, CUT)
        slot = wg.at[p // 2, rows_of(block, OWN), cut]
        own = stream == 0 and step == 0
        to = {"z": z_up if way == 0 else z_down}
        at = (stream, way, step)
        copies = [remote(wts.at[p // 2, :, cut] if own else slot, slot, w_ss.at[at + (p,)], w_rs.at[at + (p,)], to)]
        if p == 0:
            slot = coef.at[rows_of(block, OWN), :]
            copies.append(remote(coef_own if own else slot, slot, c_ss.at[at], c_rs.at[at], to))
        return copies

    def unit(source, u):
        return tk.at[pl.ds(pl.multiple_of(source * POS + core * (POS // 2) + u * UNIT, UNIT), UNIT), :]

    def near(way, u):
        src = tok.at[pl.ds(pl.multiple_of(core * (POS // 2) + u * UNIT, UNIT), UNIT), :]
        to = {"x": x_up if way == 0 else x_down}
        return [remote(src, unit(x, u), t_ss.at[way, u], t_rs.at[way, u], to)]

    def far(way):
        to = {"x": x_up if way == 0 else x_down}
        src = unit(x_down if way == 0 else x_up, way)
        return [remote(src, src, t_ss.at[way, 2], t_rs.at[way, 2], to)]

    def pass_on(index, source, u):
        src = unit(source, u)
        return [remote(src, src, p_ss.at[index], p_rs.at[index], {"c": 1 - core})]

    def to_mate(p):
        cut = pl.ds(p % 2 * CUT, CUT)
        copies = [remote(
            wts.at[p // 2, :, cut], wg.at[p // 2, rows_of(me, OWN), cut], h_ss.at[p], h_rs.at[p], {"h": 1 - h}
        )]
        if p == 0:
            copies.append(remote(coef_own, coef.at[rows_of(me, OWN), :], h_ss.at[CHUNKS], h_rs.at[CHUNKS], {"h": 1 - h}))
        return copies

    flying = {}
    for p in range(CHUNKS):
        for way in (0, 1):
            flying["ring", 0, way, 0, p] = launch(ring(0, way, 0, p))
        flying["mate", p] = launch(to_mate(p))
    for way, u in ((0, 0), (1, 1), (0, 1), (1, 0)):
        flying["near", way, u] = launch(near(way, u))
    cots = launch([
        remote(cot.at[:, lax.rem(x + i, X)], cotv.at[x], ct_ss.at[i - 1], ct_rs.at[i - 1], {"x": lax.rem(x + i, X)})
        for i in range(1, X)
    ])
    def turn_cotangent(i, carry):
        cot_s[rows_of(i, POS), :] = jnp.transpose(cotv[i].astype(F32).reshape(CH, POS))
        return carry

    order = arrival_order()
    last_coef = max(i for i, message in enumerate(order) if message[0] == "ring" and message[4] == 0)
    for i, message in enumerate(order):
        arrived(flying[message])
        if message[0] == "ring":
            _, stream, way, step, p = message
            if step + 1 < STEPS[stream][way]:
                flying["ring", stream, way, step + 1, p] = launch(ring(stream, way, step + 1, p))
        elif message[0] == "mate":
            for way in (0, 1):
                flying["ring", 1, way, 0, message[1]] = launch(ring(1, way, 0, message[1]))
        elif message[0] == "near":
            _, way, u = message
            if u == way:
                flying["far", way] = launch(far(way))
            flying["pass", 2 * way + u] = launch(pass_on(2 * way + u, x_down if way == 0 else x_up, u))
        elif message[0] == "far":
            way = message[1]
            flying["pass", 4 + way] = launch(pass_on(4 + way, x_far, way))
        if i == len(order) * 2 // 3:
            arrived(cots)
            for copy in local:
                copy.wait()
            lax.fori_loop(0, X, turn_cotangent, 0)
        if i == last_coef:
            by_mode = jnp.transpose(coef[...])
            residue, decay = by_mode[0:M, :], by_mode[M:2 * M, :]
            width = jnp.sqrt(2.0 * decay)
            once, scaled = jnp.exp(-decay), residue * width
            for m in range(M):
                a_t[m] = jnp.broadcast_to(once[m:m + 1, :], (8, CH))
                r_t[m] = jnp.broadcast_to(scaled[m:m + 1, :], (8, CH))

    def project(i, carry):
        out = lax.dot_general(
            tk[rows_of(i, POS), :], wg[...].reshape(3 * CH, D),
            (((1,), (1,)), ((), ())), preferred_element_type=F32,
        )
        q_s[rows_of(i, POS), :] = rounded(out[:, 0:CH])
        k_s[rows_of(i, POS), :] = rounded(out[:, CH:2 * CH])
        v_s[rows_of(i, POS), :] = rounded(out[:, 2 * CH:3 * CH])
        return carry

    lax.fori_loop(0, X, project, 0)

    def gate(i, carry):
        at = rows_of(i, POS)
        g_s[at, :] = rounded(k_s[at, :] * v_s[at, :])
        s_s[at, :] = rounded(cot_s[at, :] * q_s[at, :])
        return carry

    lax.fori_loop(0, X, gate, 0)

    def states(t, carry):
        up, down = carry
        g_now = g_s[pl.ds(t, 8, stride=SUB), :]
        s_now = s_s[pl.ds(SUB - 1 - t, 8, stride=SUB), :]
        return (
            tuple(a_t[m] * up[m] + g_now for m in range(M)),
            tuple(a_t[m] * down[m] + s_now for m in range(M)),
        )

    zero = tuple(jnp.zeros((8, CH), F32) for _ in range(M))
    up, down = lax.fori_loop(0, SUB, states, (zero, zero))
    piece = lax.broadcasted_iota(jnp.int32, (8, CH), 0)
    for m in range(M):
        lost = decay[m:m + 1, :]
        fore, aft = up[m], down[m]
        for shift in (1, 2, 4):
            keep = jnp.exp(lost * (-float(SUB * shift)))
            fore = fore + jnp.where(piece >= shift, keep * pltpu.roll(fore, shift, 0), 0.0)
            aft = aft + jnp.where(piece < 8 - shift, keep * pltpu.roll(aft, 8 - shift, 0), 0.0)
        eb[0, m:m + 1, :] = fore[7:8, :]
        eb[1, m:m + 1, :] = aft[0:1, :]
        cl_t[m] = jnp.where(piece >= 1, pltpu.roll(fore, 1, 0), 0.0)
        cb_t[m] = jnp.where(piece < 7, pltpu.roll(aft, 7, 0), 0.0)

    states_out = []
    for i in sorted(range(1, ZH), key=lambda i: (-(i % H), abs(i - ZH // 2))):
        to = lax.rem(me + i, ZH)
        which = jnp.where(to > me, 0, 1)
        states_out.append(remote(
            eb.at[which], st.at[me], st_ss.at[i], st_rs.at[i],
            {"z": lax.div(to, H), "h": lax.rem(to, H)},
        ))
    launch(states_out)
    arrived(states_out)

    far_keep = jnp.exp(decay * (-float(ROWS)))
    none = jnp.zeros((M, CH), F32)
    before = lax.fori_loop(0, me, lambda j, s: far_keep * s + st[j], none)
    after = lax.fori_loop(0, ZH - 1 - me, lambda j, s: far_keep * s + st[ZH - 1 - j], none)

    place = piece.astype(F32) * float(SUB)
    start_up, start_down = [], []
    for m in range(M):
        lost = decay[m:m + 1, :]
        start_up.append(cl_t[m] + jnp.exp(-lost * place) * before[m:m + 1, :])
        start_down.append(
            cb_t[m] + jnp.exp(-lost * (float(SUB * 7) - place)) * after[m:m + 1, :]
        )

    def forward(t, carry):
        up, total = carry
        at = pl.ds(t, 8, stride=SUB)
        g_now, s_now = g_s[at, :], s_s[at, :]
        up = tuple(a_t[m] * up[m] + g_now for m in range(M))
        conv_s[at, :] = tree_sum(r_t[m] * up[m] for m in range(M))
        return up, tuple(total[m] + s_now * up[m] for m in range(M))

    def backward(t, down):
        at = pl.ds(SUB - 1 - t, 8, stride=SUB)
        s_now = s_s[at, :]
        down = tuple(a_t[m] * down[m] + s_now for m in range(M))
        back_s[at, :] = tree_sum(r_t[m] * down[m] for m in range(M))
        return down

    _, total = lax.fori_loop(0, SUB, forward, (tuple(start_up), zero))
    lax.fori_loop(0, SUB, backward, tuple(start_down))

    def gates(i, carry):
        at = rows_of(i, POS)
        conv, back = rounded(conv_s[at, :]), rounded(back_s[at, :])
        g_mat[at, 0:CH] = (cot_s[at, :] * conv).astype(BF16)
        g_mat[at, CH:2 * CH] = (back * v_s[at, :]).astype(BF16)
        g_mat[at, 2 * CH:3 * CH] = (back * k_s[at, :]).astype(BF16)
        return carry

    lax.fori_loop(0, X, gates, 0)

    def outputs(i, carry):
        at = rows_of(i, POS)
        hyena = jnp.transpose(q_s[at, :] * rounded(conv_s[at, :]))
        hy_t[i] = hyena.reshape(ZH, OWN, POS).astype(BF16)
        return carry

    def send_outputs():
        lax.fori_loop(0, X, outputs, 0)
        hyenas = launch([
            remote(
                hy_t.at[lax.rem(x + i, X)], hy_o.at[:, x], hy_ss.at[i - 1], hy_rs.at[i - 1],
                {"x": lax.rem(x + i, X)},
            )
            for i in range(1, X)
        ])
        hy_o[:, x] = hy_t[x]
        gr_s[...] = jnp.zeros_like(gr_s)
        norm = 1.0 / math.sqrt(length)
        for m in range(M):
            gr_s[m:m + 1, :] = jnp.sum(total[m], axis=0, keepdims=True) * (width[m:m + 1, :] * norm)
        gr_t[...] = jnp.transpose(gr_s[...])
        owners = []
        for i in range(1, ZH):
            to = lax.rem(me + i, ZH)
            owners.append(remote(
                gr_t.at[rows_of(to, OWN), :], gr_r.at[i], gr_ss.at[i], gr_rs.at[i],
                {"z": lax.div(to, H), "h": lax.rem(to, H)},
            ))
        return hyenas, launch(owners)

    def product(j, mine):
        parity = core if mine else 1 - core
        col = pl.multiple_of((j // PARTS * NC + parity) * COLS + j % PARTS * WIDE, WIDE)

        def tile(i, carry):
            at = rows_of(i, 2 * POS)
            out = jnp.dot(
                g_mat[at, :], wg[:, :, pl.ds(col, WIDE)].reshape(3 * CH, WIDE),
                preferred_element_type=F32,
            )
            if mine:
                acc[j, at, :] = out
            else:
                d_s[j, at, :] = out.astype(BF16)
            return carry

        lax.fori_loop(0, ROWS // (2 * POS), tile, 0)

    def chip_sum(j, owner):
        at = rows_of(owner, POS)
        return acc[j, at, :] + d_r[j, at, :].astype(F32)

    cores, first, second, finals = {}, {}, {}, {}

    def stage_product(j):
        product(j, False)
        cores[j] = launch((remote(d_s.at[j], d_r.at[j], d_ss.at[j], d_rs.at[j], {"c": 1 - core}),))
        product(j, True)

    def stage_first(j):
        arrived(cores[j])
        other = chip_sum(j, x_far)
        m1_s[j, 0] = other[:, 0:HALF].astype(BF16)
        m1_s[j, 1] = other[:, HALF:WIDE].astype(BF16)
        first[j] = launch([
            remote(m1_s.at[j, w], m1_r.at[j, w], m1_ss.at[j, w], m1_rs.at[j, w], {"x": x_up if w == 0 else x_down})
            for w in (0, 1)
        ])

    def stage_second(j):
        arrived(first[j])
        for w in (0, 1):
            side = chip_sum(j, x_up if w == 0 else x_down)
            cut = slice(0, HALF) if w == 0 else slice(HALF, WIDE)
            rest = slice(HALF, WIDE) if w == 0 else slice(0, HALF)
            m2_s[j, w, :, cut] = (side[:, cut] + m1_r[j, w].astype(F32)).astype(BF16)
            m2_s[j, w, :, rest] = side[:, rest].astype(BF16)
        second[j] = launch([
            remote(m2_s.at[j, w], m2_r.at[j, w], m2_ss.at[j, w], m2_rs.at[j, w], {"x": x_up if w == 0 else x_down})
            for w in (0, 1)
        ])

    def stage_third(j):
        arrived(second[j])
        total_x = chip_sum(j, x) + m2_r[j, 0].astype(F32) + m2_r[j, 1].astype(F32)
        owner, part = j // PARTS, j % PARTS
        copy = remote(
            y_s.at[j], y_r.at[ell, part], y_ss.at[j], y_rs.at[ell, part], {"l": jnp.int32(owner)}
        )
        finals[j] = copy

        @pl.when(ell == owner)
        def _():
            y_own[part] = total_x

        @pl.when(ell != owner)
        def _():
            y_s[j] = total_x.astype(BF16)
            copy.start()

    for i in range(PIECES + 7):
        for late, stage in ((0, stage_product), (2, stage_first), (5, stage_second), (7, stage_third)):
            if 0 <= i - late < PIECES:
                stage(ORDER[i - late])
        if i == 1:
            hyenas, owners = send_outputs()

    arrived(hyenas)
    hyena_out[...] = hy_o[...]
    arrived(owners)
    share = gr_t[rows_of(me, OWN), :]
    for i in range(1, ZH):
        share = share + gr_r[i]
    grad_residue[...] = share[:, 0:M]
    for j in range(NL):
        @pl.when(ell != j)
        def _():
            for part in range(PARTS):
                piece_at = j * PARTS + part
                remote(
                    y_s.at[piece_at], y_r.at[j, part], y_ss.at[piece_at], y_rs.at[j, part], {"l": jnp.int32(j)}
                ).wait_recv()
                y_own[part] += y_r[j, part].astype(F32)
                finals[piece_at].wait_send()
    for part in range(PARTS):
        grad_input[:, part * WIDE:(part + 1) * WIDE] = y_own[part].astype(BF16)
    for copy in sends:
        copy.wait_send()


def shards(tokens, weights, residues, decay_rates, cotangent, length):
    wts = jnp.transpose(weights[0], (1, 0, 2))
    cot = cotangent.reshape(ZH, X, OWN, POS)
    dma = pltpu.SemaphoreType.DMA
    scratch = [
        pltpu.VMEM((ROWS, D), BF16),
        pltpu.VMEM((3, CH, D), BF16),
        pltpu.VMEM((OWN, 128), F32),
        pltpu.VMEM((CH, 128), F32),
        pltpu.VMEM((X, ZH, OWN, POS), BF16),
    ]
    scratch += [pltpu.VMEM((ROWS, CH), F32)] * 8
    scratch += [pltpu.VMEM((M, 8, CH), F32)] * 4
    scratch += [
        pltpu.VMEM((2, M, CH), F32),
        pltpu.VMEM((ZH, M, CH), F32),
        pltpu.VMEM((CH, CH), F32),
        pltpu.VMEM((CH, CH), F32),
        pltpu.VMEM((ZH, OWN, CH), F32),
        pltpu.VMEM((X, ZH, OWN, POS), BF16),
        pltpu.VMEM((ZH, X, OWN, POS), BF16),
        pltpu.VMEM((ROWS, 3 * CH), BF16),
        pltpu.VMEM((PIECES, ROWS, WIDE), F32),
        pltpu.VMEM((PIECES, ROWS, WIDE), BF16),
        pltpu.VMEM((PIECES, ROWS, WIDE), BF16),
        pltpu.VMEM((PIECES, 2, POS, HALF), BF16),
        pltpu.VMEM((PIECES, 2, POS, HALF), BF16),
        pltpu.VMEM((PIECES, 2, POS, WIDE), BF16),
        pltpu.VMEM((PIECES, 2, POS, WIDE), BF16),
        pltpu.VMEM((PIECES, POS, WIDE), BF16),
        pltpu.VMEM((NL, PARTS, POS, WIDE), BF16),
        pltpu.VMEM((PARTS, POS, WIDE), F32),
    ]
    steps = Z // 2
    scratch += [dma((3,))]
    for shape in (
        (2, 2, steps, CHUNKS), (2, 2, steps), (CHUNKS + 1,), (2, 3), (6,), (X - 1,), (ZH,), (ZH,), (X - 1,),
        (PIECES,), (PIECES, 2), (PIECES, 2),
    ):
        scratch += [dma(shape), dma(shape)]
    scratch += [dma((PIECES,)), dma((NL, PARTS))]
    vmem, hbm = pl.BlockSpec(memory_space=pltpu.VMEM), pl.BlockSpec(memory_space=pl.ANY)
    hyena, grad, residue = pl.pallas_call(
        functools.partial(body, length),
        out_shape=(
            jax.ShapeDtypeStruct((ZH, X, OWN, POS), BF16),
            jax.ShapeDtypeStruct((POS, COLS), BF16),
            jax.ShapeDtypeStruct((OWN, M), F32),
        ),
        in_specs=[hbm, hbm, vmem, vmem, hbm],
        out_specs=(vmem, vmem, vmem),
        scratch_shapes=scratch,
        compiler_params=pltpu.CompilerParams(
            collective_id=0, has_side_effects=True, vmem_limit_bytes=60 * 1024 * 1024
        ),
        name="hyena_block",
    )(tokens, wts, residues, decay_rates, cot)
    return (hyena.reshape(X * ZH * OWN, POS), grad, residue[None])


def solution(mesh):
    fine = Mesh(mesh.devices.reshape(SIZES), AXES)
    ctx, tp = ("z", "h", "x"), ("l", "c")

    def step(tokens, weights, residues, decay_rates, cotangent):
        return jax.shard_map(
            functools.partial(shards, length=tokens.shape[0]),
            mesh=fine,
            in_specs=(P(ctx, None), P(tp, ctx), P(tp, ctx), P(tp, ctx), P(tp, ctx)),
            out_specs=(P(tp, ctx), P(ctx, tp), P(tp, ctx)),
            check_vma=False,
        )(tokens, weights, residues, decay_rates, cotangent)

    return step
```

```python
import functools
import heapq
import math

import jax
import jax.numpy as jnp
from jax import lax
from jax.experimental import pallas as pl
from jax.experimental.pallas import tpu as pltpu
from jax.sharding import Mesh, PartitionSpec as P

AXES = ("z", "h", "x", "l", "c")
SIZES = (8, 2, 4, 4, 2)
Z, H, X, NL, NC = SIZES
ZH = Z * H
MESH = pl.DeviceIdType.MESH
F32 = jnp.float32
BF16 = jnp.bfloat16

D = 4096
POS = 128
OWN = 8
CH = ZH * OWN
ROWS = X * POS
M = 16
SUB = 64
COLS = D // (NL * NC)
PARTS = 2
WIDE = COLS // PARTS
HALF = WIDE // 2
PIECES = NL * PARTS
UNIT = POS // 4
CUT = D // 2
CHUNKS = 6
ORDER = (0, 6, 1, 7, 2, 4, 3, 5)
STEPS = ((Z // 2, Z - 1 - Z // 2), (Z - 1 - Z // 2, Z // 2))


def arrival_order():
    cost = {"z": 0.7, "h": 1.4, "x": 5.6, "c": 0.8}
    delay = {"z": 3.5, "h": 5.0, "x": 2.5, "c": 1.5}
    free, queue, order = {}, [], []

    def send(now, link, message):
        free[link] = max(now, free.get(link, 0.0)) + cost[link[0]]
        heapq.heappush(queue, (free[link] + delay[link[0]], len(order) + len(queue), message))

    for p in range(CHUNKS):
        for way in (0, 1):
            send(0.0, ("z", way), ("ring", 0, way, 0, p))
        send(0.0, ("h",), ("mate", p))
    for way in (0, 1):
        for u in (way, 1 - way):
            send(0.0, ("x", way), ("near", way, u))
    while queue:
        now, _, message = heapq.heappop(queue)
        order.append(message)
        if message[0] == "ring":
            _, stream, way, step, p = message
            if step + 1 < STEPS[stream][way]:
                send(now, ("z", way), ("ring", stream, way, step + 1, p))
        elif message[0] == "mate":
            for way in (0, 1):
                send(now, ("z", way), ("ring", 1, way, 0, message[1]))
        elif message[0] == "near":
            _, way, u = message
            if u == way:
                send(now, ("x", way), ("far", way))
            send(now, ("c",), ("pass", 2 * way + u))
        elif message[0] == "far":
            send(now, ("c",), ("pass", 4 + message[1]))
    return order


def remote(src, dst, send, recv, device):
    return pltpu.make_async_remote_copy(
        src_ref=src, dst_ref=dst, send_sem=send, recv_sem=recv,
        device_id=device, device_id_type=MESH,
    )


def rounded(value):
    return value.astype(BF16).astype(F32)


def tree_sum(terms):
    terms = list(terms)
    while len(terms) > 1:
        terms = [
            terms[i] + terms[i + 1] if i + 1 < len(terms) else terms[i]
            for i in range(0, len(terms), 2)
        ]
    return terms[0]


def rows_of(index, count):
    return pl.ds(pl.multiple_of(index * count, count), count)


def body(
    length,
    tok, wts, res, rate, cot,
    hyena_out, grad_input, grad_residue,
    tk, wg, coef_own, coef, cotv,
    q_s, k_s, v_s, g_s, s_s, cot_s, conv_s, back_s,
    a_t, r_t, cl_t, cb_t, eb, st, gr_s, gr_t, gr_r,
    hy_t, hy_o, g_mat, acc, d_s, d_r, m1_s, m1_r, m2_s, m2_r, y_s, y_r, y_own,
    loc_sem, w_ss, w_rs, c_ss, c_rs, h_ss, h_rs, t_ss, t_rs, p_ss, p_rs,
    ct_ss, ct_rs, st_ss, st_rs, gr_ss, gr_rs, hy_ss, hy_rs,
    d_ss, d_rs, m1_ss, m1_rs, m2_ss, m2_rs, y_ss, y_rs,
):
    z, h, x = lax.axis_index("z"), lax.axis_index("h"), lax.axis_index("x")
    ell, core = lax.axis_index("l"), lax.axis_index("c")
    me = z * H + h
    z_up, z_down = lax.rem(z + 1, Z), lax.rem(z + Z - 1, Z)
    x_up, x_down, x_far = lax.rem(x + 1, X), lax.rem(x + X - 1, X), lax.rem(x + 2, X)
    sends = []

    coef_own[...] = jnp.zeros_like(coef_own)
    coef_own[:, 0:M] = res[0]
    coef_own[:, M:2 * M] = rate[0]
    local = [
        pltpu.make_async_copy(tok, tk.at[rows_of(x, POS), :], loc_sem.at[0]),
        pltpu.make_async_copy(wts, wg.at[:, rows_of(me, OWN), :], loc_sem.at[1]),
        pltpu.make_async_copy(cot.at[:, x], cotv.at[x], loc_sem.at[2]),
    ]
    for copy in local:
        copy.start()
    coef[rows_of(me, OWN), :] = coef_own[...]

    barrier = pltpu.get_barrier_semaphore()
    peers = [{"z": z_up}, {"z": z_down}, {"h": 1 - h}, {"c": 1 - core}]
    peers += [{"x": lax.rem(x + i, X)} for i in range(1, X)]
    peers += [{"l": lax.rem(ell + i, NL)} for i in range(1, NL)]
    for peer in peers:
        pl.semaphore_signal(barrier, inc=1, device_id=peer, device_id_type=MESH)
    pl.semaphore_wait(barrier, len(peers))

    def launch(copies):
        for copy in copies:
            copy.start()
            sends.append(copy)
        return copies

    def arrived(copies):
        for copy in copies:
            copy.wait_recv()

    def ring(stream, way, step, p):
        from_z = lax.rem(z - step + Z, Z) if way == 0 else lax.rem(z + step, Z)
        block = from_z * H + (h if stream == 0 else 1 - h)
        cut = pl.ds(p % 2 * CUT, CUT)
        slot = wg.at[p // 2, rows_of(block, OWN), cut]
        own = stream == 0 and step == 0
        to = {"z": z_up if way == 0 else z_down}
        at = (stream, way, step)
        copies = [remote(wts.at[p // 2, :, cut] if own else slot, slot, w_ss.at[at + (p,)], w_rs.at[at + (p,)], to)]
        if p == 0:
            slot = coef.at[rows_of(block, OWN), :]
            copies.append(remote(coef_own if own else slot, slot, c_ss.at[at], c_rs.at[at], to))
        return copies

    def unit(source, u):
        return tk.at[pl.ds(pl.multiple_of(source * POS + core * (POS // 2) + u * UNIT, UNIT), UNIT), :]

    def near(way, u):
        src = tok.at[pl.ds(pl.multiple_of(core * (POS // 2) + u * UNIT, UNIT), UNIT), :]
        to = {"x": x_up if way == 0 else x_down}
        return [remote(src, unit(x, u), t_ss.at[way, u], t_rs.at[way, u], to)]

    def far(way):
        to = {"x": x_up if way == 0 else x_down}
        src = unit(x_down if way == 0 else x_up, way)
        return [remote(src, src, t_ss.at[way, 2], t_rs.at[way, 2], to)]

    def pass_on(index, source, u):
        src = unit(source, u)
        return [remote(src, src, p_ss.at[index], p_rs.at[index], {"c": 1 - core})]

    def to_mate(p):
        cut = pl.ds(p % 2 * CUT, CUT)
        copies = [remote(
            wts.at[p // 2, :, cut], wg.at[p // 2, rows_of(me, OWN), cut], h_ss.at[p], h_rs.at[p], {"h": 1 - h}
        )]
        if p == 0:
            copies.append(remote(coef_own, coef.at[rows_of(me, OWN), :], h_ss.at[CHUNKS], h_rs.at[CHUNKS], {"h": 1 - h}))
        return copies

    flying = {}
    for p in range(CHUNKS):
        for way in (0, 1):
            flying["ring", 0, way, 0, p] = launch(ring(0, way, 0, p))
        flying["mate", p] = launch(to_mate(p))
    for way, u in ((0, 0), (1, 1), (0, 1), (1, 0)):
        flying["near", way, u] = launch(near(way, u))
    cots = launch([
        remote(cot.at[:, lax.rem(x + i, X)], cotv.at[x], ct_ss.at[i - 1], ct_rs.at[i - 1], {"x": lax.rem(x + i, X)})
        for i in range(1, X)
    ])
    def turn_cotangent(i, carry):
        cot_s[rows_of(i, POS), :] = jnp.transpose(cotv[i].astype(F32).reshape(CH, POS))
        return carry

    order = arrival_order()
    last_coef = max(i for i, message in enumerate(order) if message[0] == "ring" and message[4] == 0)
    for i, message in enumerate(order):
        arrived(flying[message])
        if message[0] == "ring":
            _, stream, way, step, p = message
            if step + 1 < STEPS[stream][way]:
                flying["ring", stream, way, step + 1, p] = launch(ring(stream, way, step + 1, p))
        elif message[0] == "mate":
            for way in (0, 1):
                flying["ring", 1, way, 0, message[1]] = launch(ring(1, way, 0, message[1]))
        elif message[0] == "near":
            _, way, u = message
            if u == way:
                flying["far", way] = launch(far(way))
            flying["pass", 2 * way + u] = launch(pass_on(2 * way + u, x_down if way == 0 else x_up, u))
        elif message[0] == "far":
            way = message[1]
            flying["pass", 4 + way] = launch(pass_on(4 + way, x_far, way))
        if i == len(order) * 2 // 3:
            arrived(cots)
            for copy in local:
                copy.wait()
            lax.fori_loop(0, X, turn_cotangent, 0)
        if i == last_coef:
            by_mode = jnp.transpose(coef[...])
            residue, decay = by_mode[0:M, :], by_mode[M:2 * M, :]
            width = jnp.sqrt(2.0 * decay)
            once, scaled = jnp.exp(-decay), residue * width
            for m in range(M):
                a_t[m] = jnp.broadcast_to(once[m:m + 1, :], (8, CH))
                r_t[m] = jnp.broadcast_to(scaled[m:m + 1, :], (8, CH))

    def project(i, carry):
        out = lax.dot_general(
            tk[rows_of(i, POS), :], wg[...].reshape(3 * CH, D),
            (((1,), (1,)), ((), ())), preferred_element_type=F32,
        )
        q_s[rows_of(i, POS), :] = rounded(out[:, 0:CH])
        k_s[rows_of(i, POS), :] = rounded(out[:, CH:2 * CH])
        v_s[rows_of(i, POS), :] = rounded(out[:, 2 * CH:3 * CH])
        return carry

    lax.fori_loop(0, X, project, 0)

    def gate(i, carry):
        at = rows_of(i, POS)
        g_s[at, :] = rounded(k_s[at, :] * v_s[at, :])
        s_s[at, :] = rounded(cot_s[at, :] * q_s[at, :])
        return carry

    lax.fori_loop(0, X, gate, 0)

    def states(t, carry):
        up, down = carry
        g_now = g_s[pl.ds(t, 8, stride=SUB), :]
        s_now = s_s[pl.ds(SUB - 1 - t, 8, stride=SUB), :]
        return (
            tuple(a_t[m] * up[m] + g_now for m in range(M)),
            tuple(a_t[m] * down[m] + s_now for m in range(M)),
        )

    zero = tuple(jnp.zeros((8, CH), F32) for _ in range(M))
    up, down = lax.fori_loop(0, SUB, states, (zero, zero))
    piece = lax.broadcasted_iota(jnp.int32, (8, CH), 0)
    for m in range(M):
        lost = decay[m:m + 1, :]
        fore, aft = up[m], down[m]
        for shift in (1, 2, 4):
            keep = jnp.exp(lost * (-float(SUB * shift)))
            fore = fore + jnp.where(piece >= shift, keep * pltpu.roll(fore, shift, 0), 0.0)
            aft = aft + jnp.where(piece < 8 - shift, keep * pltpu.roll(aft, 8 - shift, 0), 0.0)
        eb[0, m:m + 1, :] = fore[7:8, :]
        eb[1, m:m + 1, :] = aft[0:1, :]
        cl_t[m] = jnp.where(piece >= 1, pltpu.roll(fore, 1, 0), 0.0)
        cb_t[m] = jnp.where(piece < 7, pltpu.roll(aft, 7, 0), 0.0)

    states_out = []
    for i in sorted(range(1, ZH), key=lambda i: (-(i % H), abs(i - ZH // 2))):
        to = lax.rem(me + i, ZH)
        which = jnp.where(to > me, 0, 1)
        states_out.append(remote(
            eb.at[which], st.at[me], st_ss.at[i], st_rs.at[i],
            {"z": lax.div(to, H), "h": lax.rem(to, H)},
        ))
    launch(states_out)
    arrived(states_out)

    far_keep = jnp.exp(decay * (-float(ROWS)))
    none = jnp.zeros((M, CH), F32)
    before = lax.fori_loop(0, me, lambda j, s: far_keep * s + st[j], none)
    after = lax.fori_loop(0, ZH - 1 - me, lambda j, s: far_keep * s + st[ZH - 1 - j], none)

    place = piece.astype(F32) * float(SUB)
    start_up, start_down = [], []
    for m in range(M):
        lost = decay[m:m + 1, :]
        start_up.append(cl_t[m] + jnp.exp(-lost * place) * before[m:m + 1, :])
        start_down.append(
            cb_t[m] + jnp.exp(-lost * (float(SUB * 7) - place)) * after[m:m + 1, :]
        )

    def forward(t, carry):
        up, total = carry
        at = pl.ds(t, 8, stride=SUB)
        g_now, s_now = g_s[at, :], s_s[at, :]
        up = tuple(a_t[m] * up[m] + g_now for m in range(M))
        conv_s[at, :] = tree_sum(r_t[m] * up[m] for m in range(M))
        return up, tuple(total[m] + s_now * up[m] for m in range(M))

    def backward(t, down):
        at = pl.ds(SUB - 1 - t, 8, stride=SUB)
        s_now = s_s[at, :]
        down = tuple(a_t[m] * down[m] + s_now for m in range(M))
        back_s[at, :] = tree_sum(r_t[m] * down[m] for m in range(M))
        return down

    _, total = lax.fori_loop(0, SUB, forward, (tuple(start_up), zero))
    lax.fori_loop(0, SUB, backward, tuple(start_down))

    def gates(i, carry):
        at = rows_of(i, POS)
        conv, back = rounded(conv_s[at, :]), rounded(back_s[at, :])
        g_mat[at, 0:CH] = (cot_s[at, :] * conv).astype(BF16)
        g_mat[at, CH:2 * CH] = (back * v_s[at, :]).astype(BF16)
        g_mat[at, 2 * CH:3 * CH] = (back * k_s[at, :]).astype(BF16)
        return carry

    lax.fori_loop(0, X, gates, 0)

    def outputs(i, carry):
        at = rows_of(i, POS)
        hyena = jnp.transpose(q_s[at, :] * rounded(conv_s[at, :]))
        hy_t[i] = hyena.reshape(ZH, OWN, POS).astype(BF16)
        return carry

    def send_outputs():
        lax.fori_loop(0, X, outputs, 0)
        hyenas = launch([
            remote(
                hy_t.at[lax.rem(x + i, X)], hy_o.at[:, x], hy_ss.at[i - 1], hy_rs.at[i - 1],
                {"x": lax.rem(x + i, X)},
            )
            for i in range(1, X)
        ])
        hy_o[:, x] = hy_t[x]
        gr_s[...] = jnp.zeros_like(gr_s)
        norm = 1.0 / math.sqrt(length)
        for m in range(M):
            gr_s[m:m + 1, :] = jnp.sum(total[m], axis=0, keepdims=True) * (width[m:m + 1, :] * norm)
        gr_t[...] = jnp.transpose(gr_s[...])
        owners = []
        for i in range(1, ZH):
            to = lax.rem(me + i, ZH)
            owners.append(remote(
                gr_t.at[rows_of(to, OWN), :], gr_r.at[i], gr_ss.at[i], gr_rs.at[i],
                {"z": lax.div(to, H), "h": lax.rem(to, H)},
            ))
        return hyenas, launch(owners)

    def product(j, mine):
        parity = core if mine else 1 - core
        col = pl.multiple_of((j // PARTS * NC + parity) * COLS + j % PARTS * WIDE, WIDE)

        def tile(i, carry):
            at = rows_of(i, 2 * POS)
            out = jnp.dot(
                g_mat[at, :], wg[:, :, pl.ds(col, WIDE)].reshape(3 * CH, WIDE),
                preferred_element_type=F32,
            )
            if mine:
                acc[j, at, :] = out
            else:
                d_s[j, at, :] = out.astype(BF16)
            return carry

        lax.fori_loop(0, ROWS // (2 * POS), tile, 0)

    def chip_sum(j, owner):
        at = rows_of(owner, POS)
        return acc[j, at, :] + d_r[j, at, :].astype(F32)

    cores, first, second, finals = {}, {}, {}, {}

    def stage_product(j):
        product(j, False)
        cores[j] = launch((remote(d_s.at[j], d_r.at[j], d_ss.at[j], d_rs.at[j], {"c": 1 - core}),))
        product(j, True)

    def stage_first(j):
        arrived(cores[j])
        other = chip_sum(j, x_far)
        m1_s[j, 0] = other[:, 0:HALF].astype(BF16)
        m1_s[j, 1] = other[:, HALF:WIDE].astype(BF16)
        first[j] = launch([
            remote(m1_s.at[j, w], m1_r.at[j, w], m1_ss.at[j, w], m1_rs.at[j, w], {"x": x_up if w == 0 else x_down})
            for w in (0, 1)
        ])

    def stage_second(j):
        arrived(first[j])
        for w in (0, 1):
            side = chip_sum(j, x_up if w == 0 else x_down)
            cut = slice(0, HALF) if w == 0 else slice(HALF, WIDE)
            rest = slice(HALF, WIDE) if w == 0 else slice(0, HALF)
            m2_s[j, w, :, cut] = (side[:, cut] + m1_r[j, w].astype(F32)).astype(BF16)
            m2_s[j, w, :, rest] = side[:, rest].astype(BF16)
        second[j] = launch([
            remote(m2_s.at[j, w], m2_r.at[j, w], m2_ss.at[j, w], m2_rs.at[j, w], {"x": x_up if w == 0 else x_down})
            for w in (0, 1)
        ])

    def stage_third(j):
        arrived(second[j])
        total_x = chip_sum(j, x) + m2_r[j, 0].astype(F32) + m2_r[j, 1].astype(F32)
        owner, part = j // PARTS, j % PARTS
        copy = remote(
            y_s.at[j], y_r.at[ell, part], y_ss.at[j], y_rs.at[ell, part], {"l": jnp.int32(owner)}
        )
        finals[j] = copy

        @pl.when(ell == owner)
        def _():
            y_own[part] = total_x

        @pl.when(ell != owner)
        def _():
            y_s[j] = total_x.astype(BF16)
            copy.start()

    for i in range(PIECES + 7):
        for late, stage in ((0, stage_product), (2, stage_first), (5, stage_second), (7, stage_third)):
            if 0 <= i - late < PIECES:
                stage(ORDER[i - late])
        if i == 1:
            hyenas, owners = send_outputs()

    arrived(hyenas)
    hyena_out[...] = hy_o[...]
    arrived(owners)
    share = gr_t[rows_of(me, OWN), :]
    for i in range(1, ZH):
        share = share + gr_r[i]
    grad_residue[...] = share[:, 0:M]
    for j in range(NL):
        @pl.when(ell != j)
        def _():
            for part in range(PARTS):
                piece_at = j * PARTS + part
                remote(
                    y_s.at[piece_at], y_r.at[j, part], y_ss.at[piece_at], y_rs.at[j, part], {"l": jnp.int32(j)}
                ).wait_recv()
                y_own[part] += y_r[j, part].astype(F32)
                finals[piece_at].wait_send()
    for part in range(PARTS):
        grad_input[:, part * WIDE:(part + 1) * WIDE] = y_own[part].astype(BF16)
    for copy in sends:
        copy.wait_send()


def hand_over(hyena, grad, residue, hyena_out, grad_out, residue_out):
    hyena_out[...] = hyena[...]
    grad_out[...] = grad[...]
    residue_out[...] = residue[...]


def shards(tokens, weights, residues, decay_rates, cotangent, length):
    wts = jnp.transpose(weights[0], (1, 0, 2))
    cot = cotangent.reshape(ZH, X, OWN, POS)
    dma = pltpu.SemaphoreType.DMA
    scratch = [
        pltpu.VMEM((ROWS, D), BF16),
        pltpu.VMEM((3, CH, D), BF16),
        pltpu.VMEM((OWN, 128), F32),
        pltpu.VMEM((CH, 128), F32),
        pltpu.VMEM((X, ZH, OWN, POS), BF16),
    ]
    scratch += [pltpu.VMEM((ROWS, CH), F32)] * 8
    scratch += [pltpu.VMEM((M, 8, CH), F32)] * 4
    scratch += [
        pltpu.VMEM((2, M, CH), F32),
        pltpu.VMEM((ZH, M, CH), F32),
        pltpu.VMEM((CH, CH), F32),
        pltpu.VMEM((CH, CH), F32),
        pltpu.VMEM((ZH, OWN, CH), F32),
        pltpu.VMEM((X, ZH, OWN, POS), BF16),
        pltpu.VMEM((ZH, X, OWN, POS), BF16),
        pltpu.VMEM((ROWS, 3 * CH), BF16),
        pltpu.VMEM((PIECES, ROWS, WIDE), F32),
        pltpu.VMEM((PIECES, ROWS, WIDE), BF16),
        pltpu.VMEM((PIECES, ROWS, WIDE), BF16),
        pltpu.VMEM((PIECES, 2, POS, HALF), BF16),
        pltpu.VMEM((PIECES, 2, POS, HALF), BF16),
        pltpu.VMEM((PIECES, 2, POS, WIDE), BF16),
        pltpu.VMEM((PIECES, 2, POS, WIDE), BF16),
        pltpu.VMEM((PIECES, POS, WIDE), BF16),
        pltpu.VMEM((NL, PARTS, POS, WIDE), BF16),
        pltpu.VMEM((PARTS, POS, WIDE), F32),
    ]
    steps = Z // 2
    scratch += [dma((3,))]
    for shape in (
        (2, 2, steps, CHUNKS), (2, 2, steps), (CHUNKS + 1,), (2, 3), (6,), (X - 1,), (ZH,), (ZH,), (X - 1,),
        (PIECES,), (PIECES, 2), (PIECES, 2),
    ):
        scratch += [dma(shape), dma(shape)]
    scratch += [dma((PIECES,)), dma((NL, PARTS))]
    vmem, hbm = pl.BlockSpec(memory_space=pltpu.VMEM), pl.BlockSpec(memory_space=pl.ANY)
    hyena, grad, residue = pl.pallas_call(
        functools.partial(body, length),
        out_shape=(
            pltpu.VMEM((ZH, X, OWN, POS), BF16),
            pltpu.VMEM((POS, COLS), BF16),
            pltpu.VMEM((OWN, M), F32),
        ),
        in_specs=[hbm, hbm, vmem, vmem, hbm],
        out_specs=(vmem, vmem, vmem),
        scratch_shapes=scratch,
        compiler_params=pltpu.CompilerParams(
            collective_id=0, has_side_effects=True, vmem_limit_bytes=60 * 1024 * 1024
        ),
        name="hyena_block",
    )(tokens, wts, residues, decay_rates, cot)
    hyena, grad, residue = pl.pallas_call(
        hand_over,
        out_shape=(
            jax.ShapeDtypeStruct((ZH, X, OWN, POS), BF16),
            jax.ShapeDtypeStruct((POS, COLS), BF16),
            jax.ShapeDtypeStruct((OWN, M), F32),
        ),
        in_specs=[vmem, vmem, vmem],
        out_specs=(vmem, vmem, vmem),
        compiler_params=pltpu.CompilerParams(vmem_limit_bytes=4 * 1024 * 1024),
        name="results",
    )(hyena, grad, residue)
    return (hyena.reshape(X * ZH * OWN, POS), grad, residue[None])


def solution(mesh):
    fine = Mesh(mesh.devices.reshape(SIZES), AXES)
    ctx, tp = ("z", "h", "x"), ("l", "c")

    def step(tokens, weights, residues, decay_rates, cotangent):
        return jax.shard_map(
            functools.partial(shards, length=tokens.shape[0]),
            mesh=fine,
            in_specs=(P(ctx, None), P(tp, ctx), P(tp, ctx), P(tp, ctx), P(tp, ctx)),
            out_specs=(P(tp, ctx), P(ctx, tp), P(tp, ctx)),
            check_vma=False,
        )(tokens, weights, residues, decay_rates, cotangent)

    return step
```

```python
import functools
import heapq
import math

import jax
import jax.numpy as jnp
from jax import lax
from jax.experimental import pallas as pl
from jax.experimental.pallas import tpu as pltpu
from jax.sharding import Mesh, PartitionSpec as P

AXES = ("z", "h", "x", "l", "c")
SIZES = (8, 2, 4, 4, 2)
Z, H, X, NL, NC = SIZES
ZH = Z * H
MESH = pl.DeviceIdType.MESH
F32 = jnp.float32
BF16 = jnp.bfloat16

D = 4096
POS = 128
OWN = 8
CH = ZH * OWN
ROWS = X * POS
M = 16
SUB = 64
COLS = D // (NL * NC)
PARTS = 2
WIDE = COLS // PARTS
HALF = WIDE // 2
PIECES = NL * PARTS
UNIT = POS // 4
CUT = D // 2
CHUNKS = 6
ORDER = (0, 6, 1, 7, 2, 4, 3, 5)
STEPS = ((Z // 2, Z - 1 - Z // 2), (Z - 1 - Z // 2, Z // 2))


def arrival_order():
    cost = {"z": 0.7, "h": 1.4, "x": 5.6, "c": 0.8}
    delay = {"z": 3.5, "h": 5.0, "x": 2.5, "c": 1.5}
    free, queue, order = {}, [], []

    def send(now, link, message):
        free[link] = max(now, free.get(link, 0.0)) + cost[link[0]]
        heapq.heappush(queue, (free[link] + delay[link[0]], len(order) + len(queue), message))

    for p in range(CHUNKS):
        for way in (0, 1):
            send(0.0, ("z", way), ("ring", 0, way, 0, p))
        send(0.0, ("h",), ("mate", p))
    for way in (0, 1):
        for u in (way, 1 - way):
            send(0.0, ("x", way), ("near", way, u))
    while queue:
        now, _, message = heapq.heappop(queue)
        order.append(message)
        if message[0] == "ring":
            _, stream, way, step, p = message
            if step + 1 < STEPS[stream][way]:
                send(now, ("z", way), ("ring", stream, way, step + 1, p))
        elif message[0] == "mate":
            for way in (0, 1):
                send(now, ("z", way), ("ring", 1, way, 0, message[1]))
        elif message[0] == "near":
            _, way, u = message
            if u == way:
                send(now, ("x", way), ("far", way))
            send(now, ("c",), ("pass", 2 * way + u))
        elif message[0] == "far":
            send(now, ("c",), ("pass", 4 + message[1]))
    return order


def remote(src, dst, send, recv, device):
    return pltpu.make_async_remote_copy(
        src_ref=src, dst_ref=dst, send_sem=send, recv_sem=recv,
        device_id=device, device_id_type=MESH,
    )


def rounded(value):
    return value.astype(BF16).astype(F32)


def tree_sum(terms):
    terms = list(terms)
    while len(terms) > 1:
        terms = [
            terms[i] + terms[i + 1] if i + 1 < len(terms) else terms[i]
            for i in range(0, len(terms), 2)
        ]
    return terms[0]


def rows_of(index, count):
    return pl.ds(pl.multiple_of(index * count, count), count)


def body(
    length,
    tok, wts, res, rate, cot,
    hyena_out, grad_input, grad_residue,
    tk, wg, coef_own, coef, cotv,
    q_s, k_s, v_s, g_s, s_s, cot_s, conv_s, back_s,
    a_t, r_t, cl_t, cb_t, eb, st, gr_s, gr_t, gr_r,
    hy_t, hy_o, g_mat, acc, d_s, d_r, m1_s, m1_r, m2_s, m2_r, y_s, y_r, y_own,
    loc_sem, w_ss, w_rs, c_ss, c_rs, h_ss, h_rs, t_ss, t_rs, p_ss, p_rs,
    ct_ss, ct_rs, st_ss, st_rs, gr_ss, gr_rs, hy_ss, hy_rs,
    d_ss, d_rs, m1_ss, m1_rs, m2_ss, m2_rs, y_ss, y_rs,
):
    z, h, x = lax.axis_index("z"), lax.axis_index("h"), lax.axis_index("x")
    ell, core = lax.axis_index("l"), lax.axis_index("c")
    me = z * H + h
    z_up, z_down = lax.rem(z + 1, Z), lax.rem(z + Z - 1, Z)
    x_up, x_down, x_far = lax.rem(x + 1, X), lax.rem(x + X - 1, X), lax.rem(x + 2, X)
    sends = []

    coef_own[...] = jnp.zeros_like(coef_own)
    coef_own[:, 0:M] = res[0]
    coef_own[:, M:2 * M] = rate[0]
    local = [
        pltpu.make_async_copy(tok, tk.at[rows_of(x, POS), :], loc_sem.at[0]),
        pltpu.make_async_copy(wts, wg.at[:, rows_of(me, OWN), :], loc_sem.at[1]),
        pltpu.make_async_copy(cot.at[:, x], cotv.at[x], loc_sem.at[2]),
    ]
    for copy in local:
        copy.start()
    coef[rows_of(me, OWN), :] = coef_own[...]

    barrier = pltpu.get_barrier_semaphore()
    peers = [{"z": z_up}, {"z": z_down}, {"h": 1 - h}, {"c": 1 - core}]
    peers += [{"x": lax.rem(x + i, X)} for i in range(1, X)]
    peers += [{"l": lax.rem(ell + i, NL)} for i in range(1, NL)]
    for peer in peers:
        pl.semaphore_signal(barrier, inc=1, device_id=peer, device_id_type=MESH)
    pl.semaphore_wait(barrier, len(peers))

    def launch(copies):
        for copy in copies:
            copy.start()
            sends.append(copy)
        return copies

    def arrived(copies):
        for copy in copies:
            copy.wait_recv()

    def ring(stream, way, step, p):
        from_z = lax.rem(z - step + Z, Z) if way == 0 else lax.rem(z + step, Z)
        block = from_z * H + (h if stream == 0 else 1 - h)
        cut = pl.ds(p % 2 * CUT, CUT)
        slot = wg.at[p // 2, rows_of(block, OWN), cut]
        own = stream == 0 and step == 0
        to = {"z": z_up if way == 0 else z_down}
        at = (stream, way, step)
        copies = [remote(wts.at[p // 2, :, cut] if own else slot, slot, w_ss.at[at + (p,)], w_rs.at[at + (p,)], to)]
        if p == 0:
            slot = coef.at[rows_of(block, OWN), :]
            copies.append(remote(coef_own if own else slot, slot, c_ss.at[at], c_rs.at[at], to))
        return copies

    def unit(source, u):
        return tk.at[pl.ds(pl.multiple_of(source * POS + core * (POS // 2) + u * UNIT, UNIT), UNIT), :]

    def near(way, u):
        src = tok.at[pl.ds(pl.multiple_of(core * (POS // 2) + u * UNIT, UNIT), UNIT), :]
        to = {"x": x_up if way == 0 else x_down}
        return [remote(src, unit(x, u), t_ss.at[way, u], t_rs.at[way, u], to)]

    def far(way):
        to = {"x": x_up if way == 0 else x_down}
        src = unit(x_down if way == 0 else x_up, way)
        return [remote(src, src, t_ss.at[way, 2], t_rs.at[way, 2], to)]

    def pass_on(index, source, u):
        src = unit(source, u)
        return [remote(src, src, p_ss.at[index], p_rs.at[index], {"c": 1 - core})]

    def to_mate(p):
        cut = pl.ds(p % 2 * CUT, CUT)
        copies = [remote(
            wts.at[p // 2, :, cut], wg.at[p // 2, rows_of(me, OWN), cut], h_ss.at[p], h_rs.at[p], {"h": 1 - h}
        )]
        if p == 0:
            copies.append(remote(coef_own, coef.at[rows_of(me, OWN), :], h_ss.at[CHUNKS], h_rs.at[CHUNKS], {"h": 1 - h}))
        return copies

    flying = {}
    for p in range(CHUNKS):
        for way in (0, 1):
            flying["ring", 0, way, 0, p] = launch(ring(0, way, 0, p))
        flying["mate", p] = launch(to_mate(p))
    for way, u in ((0, 0), (1, 1), (0, 1), (1, 0)):
        flying["near", way, u] = launch(near(way, u))
    cots = launch([
        remote(cot.at[:, lax.rem(x + i, X)], cotv.at[x], ct_ss.at[i - 1], ct_rs.at[i - 1], {"x": lax.rem(x + i, X)})
        for i in range(1, X)
    ])
    def turn_cotangent(i, carry):
        cot_s[rows_of(i, POS), :] = jnp.transpose(cotv[i].astype(F32).reshape(CH, POS))
        return carry

    order = arrival_order()
    last_coef = max(i for i, message in enumerate(order) if message[0] == "ring" and message[4] == 0)
    for i, message in enumerate(order):
        arrived(flying[message])
        if message[0] == "ring":
            _, stream, way, step, p = message
            if step + 1 < STEPS[stream][way]:
                flying["ring", stream, way, step + 1, p] = launch(ring(stream, way, step + 1, p))
        elif message[0] == "mate":
            for way in (0, 1):
                flying["ring", 1, way, 0, message[1]] = launch(ring(1, way, 0, message[1]))
        elif message[0] == "near":
            _, way, u = message
            if u == way:
                flying["far", way] = launch(far(way))
            flying["pass", 2 * way + u] = launch(pass_on(2 * way + u, x_down if way == 0 else x_up, u))
        elif message[0] == "far":
            way = message[1]
            flying["pass", 4 + way] = launch(pass_on(4 + way, x_far, way))
        if i == len(order) * 2 // 3:
            arrived(cots)
            for copy in local:
                copy.wait()
            lax.fori_loop(0, X, turn_cotangent, 0)
        if i == last_coef:
            by_mode = jnp.transpose(coef[...])
            residue, decay = by_mode[0:M, :], by_mode[M:2 * M, :]
            width = jnp.sqrt(2.0 * decay)
            once, scaled = jnp.exp(-decay), residue * width
            for m in range(M):
                a_t[m] = jnp.broadcast_to(once[m:m + 1, :], (8, CH))
                r_t[m] = jnp.broadcast_to(scaled[m:m + 1, :], (8, CH))

    def project(i, carry):
        out = lax.dot_general(
            tk[rows_of(i, ROWS // 2), :], wg[...].reshape(3 * CH, D),
            (((1,), (1,)), ((), ())), preferred_element_type=F32,
        )
        q_s[rows_of(i, ROWS // 2), :] = rounded(out[:, 0:CH])
        k_s[rows_of(i, ROWS // 2), :] = rounded(out[:, CH:2 * CH])
        v_s[rows_of(i, ROWS // 2), :] = rounded(out[:, 2 * CH:3 * CH])
        return carry

    lax.fori_loop(0, 2, project, 0)

    def gate(i, carry):
        at = rows_of(i, POS)
        g_s[at, :] = rounded(k_s[at, :] * v_s[at, :])
        s_s[at, :] = rounded(cot_s[at, :] * q_s[at, :])
        return carry

    lax.fori_loop(0, X, gate, 0)

    def states(t, carry):
        up, down = carry
        g_now = g_s[pl.ds(t, 8, stride=SUB), :]
        s_now = s_s[pl.ds(SUB - 1 - t, 8, stride=SUB), :]
        return (
            tuple(a_t[m] * up[m] + g_now for m in range(M)),
            tuple(a_t[m] * down[m] + s_now for m in range(M)),
        )

    zero = tuple(jnp.zeros((8, CH), F32) for _ in range(M))
    up, down = lax.fori_loop(0, SUB, states, (zero, zero))
    piece = lax.broadcasted_iota(jnp.int32, (8, CH), 0)
    for m in range(M):
        lost = decay[m:m + 1, :]
        fore, aft = up[m], down[m]
        for shift in (1, 2, 4):
            keep = jnp.exp(lost * (-float(SUB * shift)))
            fore = fore + jnp.where(piece >= shift, keep * pltpu.roll(fore, shift, 0), 0.0)
            aft = aft + jnp.where(piece < 8 - shift, keep * pltpu.roll(aft, 8 - shift, 0), 0.0)
        eb[0, m:m + 1, :] = fore[7:8, :]
        eb[1, m:m + 1, :] = aft[0:1, :]
        cl_t[m] = jnp.where(piece >= 1, pltpu.roll(fore, 1, 0), 0.0)
        cb_t[m] = jnp.where(piece < 7, pltpu.roll(aft, 7, 0), 0.0)

    states_out = []
    for i in sorted(range(1, ZH), key=lambda i: (-(i % H), abs(i - ZH // 2))):
        to = lax.rem(me + i, ZH)
        which = jnp.where(to > me, 0, 1)
        states_out.append(remote(
            eb.at[which], st.at[me], st_ss.at[i], st_rs.at[i],
            {"z": lax.div(to, H), "h": lax.rem(to, H)},
        ))
    launch(states_out)
    arrived(states_out)

    far_keep = jnp.exp(decay * (-float(ROWS)))
    none = jnp.zeros((M, CH), F32)
    before = lax.fori_loop(0, me, lambda j, s: far_keep * s + st[j], none)
    after = lax.fori_loop(0, ZH - 1 - me, lambda j, s: far_keep * s + st[ZH - 1 - j], none)

    place = piece.astype(F32) * float(SUB)
    start_up, start_down = [], []
    for m in range(M):
        lost = decay[m:m + 1, :]
        start_up.append(cl_t[m] + jnp.exp(-lost * place) * before[m:m + 1, :])
        start_down.append(
            cb_t[m] + jnp.exp(-lost * (float(SUB * 7) - place)) * after[m:m + 1, :]
        )

    def forward(t, carry):
        up, total = carry
        at = pl.ds(t, 8, stride=SUB)
        g_now, s_now = g_s[at, :], s_s[at, :]
        up = tuple(a_t[m] * up[m] + g_now for m in range(M))
        conv_s[at, :] = tree_sum(r_t[m] * up[m] for m in range(M))
        return up, tuple(total[m] + s_now * up[m] for m in range(M))

    def backward(t, down):
        at = pl.ds(SUB - 1 - t, 8, stride=SUB)
        s_now = s_s[at, :]
        down = tuple(a_t[m] * down[m] + s_now for m in range(M))
        back_s[at, :] = tree_sum(r_t[m] * down[m] for m in range(M))
        return down

    _, total = lax.fori_loop(0, SUB, forward, (tuple(start_up), zero))
    lax.fori_loop(0, SUB, backward, tuple(start_down))

    def gates(i, carry):
        at = rows_of(i, POS)
        conv, back = rounded(conv_s[at, :]), rounded(back_s[at, :])
        g_mat[at, 0:CH] = (cot_s[at, :] * conv).astype(BF16)
        g_mat[at, CH:2 * CH] = (back * v_s[at, :]).astype(BF16)
        g_mat[at, 2 * CH:3 * CH] = (back * k_s[at, :]).astype(BF16)
        return carry

    lax.fori_loop(0, X, gates, 0)

    def outputs(i, carry):
        at = rows_of(i, POS)
        hyena = jnp.transpose(q_s[at, :] * rounded(conv_s[at, :]))
        hy_t[i] = hyena.reshape(ZH, OWN, POS).astype(BF16)
        return carry

    def send_outputs():
        lax.fori_loop(0, X, outputs, 0)
        hyenas = launch([
            remote(
                hy_t.at[lax.rem(x + i, X)], hy_o.at[:, x], hy_ss.at[i - 1], hy_rs.at[i - 1],
                {"x": lax.rem(x + i, X)},
            )
            for i in range(1, X)
        ])
        hy_o[:, x] = hy_t[x]
        gr_s[...] = jnp.zeros_like(gr_s)
        norm = 1.0 / math.sqrt(length)
        for m in range(M):
            gr_s[m:m + 1, :] = jnp.sum(total[m], axis=0, keepdims=True) * (width[m:m + 1, :] * norm)
        gr_t[...] = jnp.transpose(gr_s[...])
        owners = []
        for i in range(1, ZH):
            to = lax.rem(me + i, ZH)
            owners.append(remote(
                gr_t.at[rows_of(to, OWN), :], gr_r.at[i], gr_ss.at[i], gr_rs.at[i],
                {"z": lax.div(to, H), "h": lax.rem(to, H)},
            ))
        return hyenas, launch(owners)

    def product(j, mine):
        parity = core if mine else 1 - core
        col = pl.multiple_of((j // PARTS * NC + parity) * COLS + j % PARTS * WIDE, WIDE)

        def tile(i, carry):
            at = rows_of(i, ROWS)
            out = jnp.dot(
                g_mat[at, :], wg[:, :, pl.ds(col, WIDE)].reshape(3 * CH, WIDE),
                preferred_element_type=F32,
            )
            if mine:
                acc[j, at, :] = out
            else:
                d_s[j, at, :] = out.astype(BF16)
            return carry

        tile(0, 0)

    def chip_sum(j, owner):
        at = rows_of(owner, POS)
        return acc[j, at, :] + d_r[j, at, :].astype(F32)

    cores, first, second, finals = {}, {}, {}, {}

    def stage_product(j):
        product(j, False)
        cores[j] = launch((remote(d_s.at[j], d_r.at[j], d_ss.at[j], d_rs.at[j], {"c": 1 - core}),))
        product(j, True)

    def stage_first(j):
        arrived(cores[j])
        other = chip_sum(j, x_far)
        m1_s[j, 0] = other[:, 0:HALF].astype(BF16)
        m1_s[j, 1] = other[:, HALF:WIDE].astype(BF16)
        first[j] = launch([
            remote(m1_s.at[j, w], m1_r.at[j, w], m1_ss.at[j, w], m1_rs.at[j, w], {"x": x_up if w == 0 else x_down})
            for w in (0, 1)
        ])

    def stage_second(j):
        arrived(first[j])
        for w in (0, 1):
            side = chip_sum(j, x_up if w == 0 else x_down)
            cut = slice(0, HALF) if w == 0 else slice(HALF, WIDE)
            rest = slice(HALF, WIDE) if w == 0 else slice(0, HALF)
            m2_s[j, w, :, cut] = (side[:, cut] + m1_r[j, w].astype(F32)).astype(BF16)
            m2_s[j, w, :, rest] = side[:, rest].astype(BF16)
        second[j] = launch([
            remote(m2_s.at[j, w], m2_r.at[j, w], m2_ss.at[j, w], m2_rs.at[j, w], {"x": x_up if w == 0 else x_down})
            for w in (0, 1)
        ])

    def stage_third(j):
        arrived(second[j])
        total_x = chip_sum(j, x) + m2_r[j, 0].astype(F32) + m2_r[j, 1].astype(F32)
        owner, part = j // PARTS, j % PARTS
        copy = remote(
            y_s.at[j], y_r.at[ell, part], y_ss.at[j], y_rs.at[ell, part], {"l": jnp.int32(owner)}
        )
        finals[j] = copy

        @pl.when(ell == owner)
        def _():
            y_own[part] = total_x

        @pl.when(ell != owner)
        def _():
            y_s[j] = total_x.astype(BF16)
            copy.start()

    for i in range(PIECES + 7):
        for late, stage in ((0, stage_product), (2, stage_first), (5, stage_second), (7, stage_third)):
            if 0 <= i - late < PIECES:
                stage(ORDER[i - late])
        if i == 1:
            hyenas, owners = send_outputs()

    arrived(hyenas)
    hyena_out[...] = hy_o[...]
    arrived(owners)
    share = gr_t[rows_of(me, OWN), :]
    for i in range(1, ZH):
        share = share + gr_r[i]
    grad_residue[...] = share[:, 0:M]
    for j in range(NL):
        @pl.when(ell != j)
        def _():
            for part in range(PARTS):
                piece_at = j * PARTS + part
                remote(
                    y_s.at[piece_at], y_r.at[j, part], y_ss.at[piece_at], y_rs.at[j, part], {"l": jnp.int32(j)}
                ).wait_recv()
                y_own[part] += y_r[j, part].astype(F32)
                finals[piece_at].wait_send()
    for part in range(PARTS):
        grad_input[:, part * WIDE:(part + 1) * WIDE] = y_own[part].astype(BF16)
    for copy in sends:
        copy.wait_send()


def hand_over(hyena, grad, residue, hyena_out, grad_out, residue_out):
    hyena_out[...] = hyena[...]
    grad_out[...] = grad[...]
    residue_out[...] = residue[...]


def shards(tokens, weights, residues, decay_rates, cotangent, length):
    wts = jnp.transpose(weights[0], (1, 0, 2))
    cot = cotangent.reshape(ZH, X, OWN, POS)
    dma = pltpu.SemaphoreType.DMA
    scratch = [
        pltpu.VMEM((ROWS, D), BF16),
        pltpu.VMEM((3, CH, D), BF16),
        pltpu.VMEM((OWN, 128), F32),
        pltpu.VMEM((CH, 128), F32),
        pltpu.VMEM((X, ZH, OWN, POS), BF16),
    ]
    scratch += [pltpu.VMEM((ROWS, CH), F32)] * 8
    scratch += [pltpu.VMEM((M, 8, CH), F32)] * 4
    scratch += [
        pltpu.VMEM((2, M, CH), F32),
        pltpu.VMEM((ZH, M, CH), F32),
        pltpu.VMEM((CH, CH), F32),
        pltpu.VMEM((CH, CH), F32),
        pltpu.VMEM((ZH, OWN, CH), F32),
        pltpu.VMEM((X, ZH, OWN, POS), BF16),
        pltpu.VMEM((ZH, X, OWN, POS), BF16),
        pltpu.VMEM((ROWS, 3 * CH), BF16),
        pltpu.VMEM((PIECES, ROWS, WIDE), F32),
        pltpu.VMEM((PIECES, ROWS, WIDE), BF16),
        pltpu.VMEM((PIECES, ROWS, WIDE), BF16),
        pltpu.VMEM((PIECES, 2, POS, HALF), BF16),
        pltpu.VMEM((PIECES, 2, POS, HALF), BF16),
        pltpu.VMEM((PIECES, 2, POS, WIDE), BF16),
        pltpu.VMEM((PIECES, 2, POS, WIDE), BF16),
        pltpu.VMEM((PIECES, POS, WIDE), BF16),
        pltpu.VMEM((NL, PARTS, POS, WIDE), BF16),
        pltpu.VMEM((PARTS, POS, WIDE), F32),
    ]
    steps = Z // 2
    scratch += [dma((3,))]
    for shape in (
        (2, 2, steps, CHUNKS), (2, 2, steps), (CHUNKS + 1,), (2, 3), (6,), (X - 1,), (ZH,), (ZH,), (X - 1,),
        (PIECES,), (PIECES, 2), (PIECES, 2),
    ):
        scratch += [dma(shape), dma(shape)]
    scratch += [dma((PIECES,)), dma((NL, PARTS))]
    vmem, hbm = pl.BlockSpec(memory_space=pltpu.VMEM), pl.BlockSpec(memory_space=pl.ANY)
    hyena, grad, residue = pl.pallas_call(
        functools.partial(body, length),
        out_shape=(
            pltpu.VMEM((ZH, X, OWN, POS), BF16),
            pltpu.VMEM((POS, COLS), BF16),
            pltpu.VMEM((OWN, M), F32),
        ),
        in_specs=[hbm, hbm, vmem, vmem, hbm],
        out_specs=(vmem, vmem, vmem),
        scratch_shapes=scratch,
        compiler_params=pltpu.CompilerParams(
            collective_id=0, has_side_effects=True, vmem_limit_bytes=60 * 1024 * 1024
        ),
        name="hyena_block",
    )(tokens, wts, residues, decay_rates, cot)
    hyena, grad, residue = pl.pallas_call(
        hand_over,
        out_shape=(
            jax.ShapeDtypeStruct((ZH, X, OWN, POS), BF16),
            jax.ShapeDtypeStruct((POS, COLS), BF16),
            jax.ShapeDtypeStruct((OWN, M), F32),
        ),
        in_specs=[vmem, vmem, vmem],
        out_specs=(vmem, vmem, vmem),
        compiler_params=pltpu.CompilerParams(vmem_limit_bytes=4 * 1024 * 1024),
        name="results",
    )(hyena, grad, residue)
    return (hyena.reshape(X * ZH * OWN, POS), grad, residue[None])


def solution(mesh):
    fine = Mesh(mesh.devices.reshape(SIZES), AXES)
    ctx, tp = ("z", "h", "x"), ("l", "c")

    def step(tokens, weights, residues, decay_rates, cotangent):
        return jax.shard_map(
            functools.partial(shards, length=tokens.shape[0]),
            mesh=fine,
            in_specs=(P(ctx, None), P(tp, ctx), P(tp, ctx), P(tp, ctx), P(tp, ctx)),
            out_specs=(P(tp, ctx), P(ctx, tp), P(tp, ctx)),
            check_vma=False,
        )(tokens, weights, residues, decay_rates, cotangent)

    return step
```

```python
import functools
import heapq
import math

import jax
import jax.numpy as jnp
from jax import lax
from jax.experimental import pallas as pl
from jax.experimental.pallas import tpu as pltpu
from jax.sharding import Mesh, PartitionSpec as P

AXES = ("z", "h", "x", "l", "c")
SIZES = (8, 2, 4, 4, 2)
Z, H, X, NL, NC = SIZES
ZH = Z * H
MESH = pl.DeviceIdType.MESH
F32 = jnp.float32
BF16 = jnp.bfloat16

D = 4096
POS = 128
OWN = 8
CH = ZH * OWN
ROWS = X * POS
M = 16
SUB = 64
COLS = D // (NL * NC)
PARTS = 2
WIDE = COLS // PARTS
HALF = WIDE // 2
PIECES = NL * PARTS
UNIT = POS // 4
CUT = D // 2
CHUNKS = 6
ORDER = (0, 6, 1, 7, 2, 4, 3, 5)
STEPS = ((Z // 2, Z - 1 - Z // 2), (Z - 1 - Z // 2, Z // 2))


def arrival_order():
    cost = {"z": 0.7, "h": 1.4, "x": 5.6, "c": 0.8}
    delay = {"z": 3.5, "h": 5.0, "x": 2.5, "c": 1.5}
    free, queue, order = {}, [], []

    def send(now, link, message):
        free[link] = max(now, free.get(link, 0.0)) + cost[link[0]]
        heapq.heappush(queue, (free[link] + delay[link[0]], len(order) + len(queue), message))

    for p in range(CHUNKS):
        for way in (0, 1):
            send(0.0, ("z", way), ("ring", 0, way, 0, p))
        send(0.0, ("h",), ("mate", p))
    for way in (0, 1):
        for u in (way, 1 - way):
            send(0.0, ("x", way), ("near", way, u))
    while queue:
        now, _, message = heapq.heappop(queue)
        order.append(message)
        if message[0] == "ring":
            _, stream, way, step, p = message
            if step + 1 < STEPS[stream][way]:
                send(now, ("z", way), ("ring", stream, way, step + 1, p))
        elif message[0] == "mate":
            for way in (0, 1):
                send(now, ("z", way), ("ring", 1, way, 0, message[1]))
        elif message[0] == "near":
            _, way, u = message
            if u == way:
                send(now, ("x", way), ("far", way))
            send(now, ("c",), ("pass", 2 * way + u))
        elif message[0] == "far":
            send(now, ("c",), ("pass", 4 + message[1]))
    return order


def remote(src, dst, send, recv, device):
    return pltpu.make_async_remote_copy(
        src_ref=src, dst_ref=dst, send_sem=send, recv_sem=recv,
        device_id=device, device_id_type=MESH,
    )


def rounded(value):
    return value.astype(BF16).astype(F32)


def tree_sum(terms):
    terms = list(terms)
    while len(terms) > 1:
        terms = [
            terms[i] + terms[i + 1] if i + 1 < len(terms) else terms[i]
            for i in range(0, len(terms), 2)
        ]
    return terms[0]


def rows_of(index, count):
    return pl.ds(pl.multiple_of(index * count, count), count)


def body(
    length,
    tok, wts, res, rate, cot,
    hyena_out, grad_input, grad_residue,
    tk, wg, coef_own, coef, cotv,
    q_s, k_s, v_s, g_s, s_s, cot_s, conv_s, back_s,
    a_t, r_t, cl_t, cb_t, eb, st, gr_s, gr_t, gr_r,
    hy_t, hy_o, g_mat, acc, d_s, d_r, m1_s, m1_r, m2_s, m2_r, y_s, y_r, y_own,
    loc_sem, w_ss, w_rs, c_ss, c_rs, h_ss, h_rs, t_ss, t_rs, p_ss, p_rs,
    ct_ss, ct_rs, st_ss, st_rs, gr_ss, gr_rs, hy_ss, hy_rs,
    d_ss, d_rs, m1_ss, m1_rs, m2_ss, m2_rs, y_ss, y_rs,
):
    z, h, x = lax.axis_index("z"), lax.axis_index("h"), lax.axis_index("x")
    ell, core = lax.axis_index("l"), lax.axis_index("c")
    me = z * H + h
    z_up, z_down = lax.rem(z + 1, Z), lax.rem(z + Z - 1, Z)
    x_up, x_down, x_far = lax.rem(x + 1, X), lax.rem(x + X - 1, X), lax.rem(x + 2, X)
    sends = []

    barrier = pltpu.get_barrier_semaphore()
    peers = [{"z": z_up}, {"z": z_down}, {"h": 1 - h}, {"c": 1 - core}]
    peers += [{"x": lax.rem(x + i, X)} for i in range(1, X)]
    peers += [{"l": lax.rem(ell + i, NL)} for i in range(1, NL)]
    for peer in peers:
        pl.semaphore_signal(barrier, inc=1, device_id=peer, device_id_type=MESH)

    coef_own[...] = jnp.zeros_like(coef_own)
    coef_own[:, 0:M] = res[0]
    coef_own[:, M:2 * M] = rate[0]
    local = [
        pltpu.make_async_copy(tok, tk.at[rows_of(x, POS), :], loc_sem.at[0]),
        pltpu.make_async_copy(wts, wg.at[:, rows_of(me, OWN), :], loc_sem.at[1]),
        pltpu.make_async_copy(cot.at[:, x], cotv.at[x], loc_sem.at[2]),
    ]
    for copy in local:
        copy.start()
    coef[rows_of(me, OWN), :] = coef_own[...]
    pl.semaphore_wait(barrier, len(peers))

    def launch(copies):
        for copy in copies:
            copy.start()
            sends.append(copy)
        return copies

    def arrived(copies):
        for copy in copies:
            copy.wait_recv()

    def ring(stream, way, step, p):
        from_z = lax.rem(z - step + Z, Z) if way == 0 else lax.rem(z + step, Z)
        block = from_z * H + (h if stream == 0 else 1 - h)
        cut = pl.ds(p % 2 * CUT, CUT)
        slot = wg.at[p // 2, rows_of(block, OWN), cut]
        own = stream == 0 and step == 0
        to = {"z": z_up if way == 0 else z_down}
        at = (stream, way, step)
        copies = [remote(wts.at[p // 2, :, cut] if own else slot, slot, w_ss.at[at + (p,)], w_rs.at[at + (p,)], to)]
        if p == 0:
            slot = coef.at[rows_of(block, OWN), :]
            copies.append(remote(coef_own if own else slot, slot, c_ss.at[at], c_rs.at[at], to))
        return copies

    def unit(source, u):
        return tk.at[pl.ds(pl.multiple_of(source * POS + core * (POS // 2) + u * UNIT, UNIT), UNIT), :]

    def near(way, u):
        src = tok.at[pl.ds(pl.multiple_of(core * (POS // 2) + u * UNIT, UNIT), UNIT), :]
        to = {"x": x_up if way == 0 else x_down}
        return [remote(src, unit(x, u), t_ss.at[way, u], t_rs.at[way, u], to)]

    def far(way):
        to = {"x": x_up if way == 0 else x_down}
        src = unit(x_down if way == 0 else x_up, way)
        return [remote(src, src, t_ss.at[way, 2], t_rs.at[way, 2], to)]

    def pass_on(index, source, u):
        src = unit(source, u)
        return [remote(src, src, p_ss.at[index], p_rs.at[index], {"c": 1 - core})]

    def to_mate(p):
        cut = pl.ds(p % 2 * CUT, CUT)
        copies = [remote(
            wts.at[p // 2, :, cut], wg.at[p // 2, rows_of(me, OWN), cut], h_ss.at[p], h_rs.at[p], {"h": 1 - h}
        )]
        if p == 0:
            copies.append(remote(coef_own, coef.at[rows_of(me, OWN), :], h_ss.at[CHUNKS], h_rs.at[CHUNKS], {"h": 1 - h}))
        return copies

    flying = {}
    for p in range(CHUNKS):
        for way in (0, 1):
            flying["ring", 0, way, 0, p] = launch(ring(0, way, 0, p))
        flying["mate", p] = launch(to_mate(p))
    for way, u in ((0, 0), (1, 1), (0, 1), (1, 0)):
        flying["near", way, u] = launch(near(way, u))
    cots = launch([
        remote(cot.at[:, lax.rem(x + i, X)], cotv.at[x], ct_ss.at[i - 1], ct_rs.at[i - 1], {"x": lax.rem(x + i, X)})
        for i in range(1, X)
    ])
    def turn_cotangent(i, carry):
        cot_s[rows_of(i, POS), :] = jnp.transpose(cotv[i].astype(F32).reshape(CH, POS))
        return carry

    order = arrival_order()
    last_coef = max(i for i, message in enumerate(order) if message[0] == "ring" and message[4] == 0)
    for i, message in enumerate(order):
        arrived(flying[message])
        if message[0] == "ring":
            _, stream, way, step, p = message
            if step + 1 < STEPS[stream][way]:
                flying["ring", stream, way, step + 1, p] = launch(ring(stream, way, step + 1, p))
        elif message[0] == "mate":
            for way in (0, 1):
                flying["ring", 1, way, 0, message[1]] = launch(ring(1, way, 0, message[1]))
        elif message[0] == "near":
            _, way, u = message
            if u == way:
                flying["far", way] = launch(far(way))
            flying["pass", 2 * way + u] = launch(pass_on(2 * way + u, x_down if way == 0 else x_up, u))
        elif message[0] == "far":
            way = message[1]
            flying["pass", 4 + way] = launch(pass_on(4 + way, x_far, way))
        if i == len(order) * 2 // 3:
            arrived(cots)
            for copy in local:
                copy.wait()
            lax.fori_loop(0, X, turn_cotangent, 0)
        if i == last_coef:
            by_mode = jnp.transpose(coef[...])
            residue, decay = by_mode[0:M, :], by_mode[M:2 * M, :]
            width = jnp.sqrt(2.0 * decay)
            once, scaled = jnp.exp(-decay), residue * width
            for m in range(M):
                a_t[m] = jnp.broadcast_to(once[m:m + 1, :], (8, CH))
                r_t[m] = jnp.broadcast_to(scaled[m:m + 1, :], (8, CH))

    def project(i, carry):
        out = lax.dot_general(
            tk[rows_of(i, ROWS // 2), :], wg[...].reshape(3 * CH, D),
            (((1,), (1,)), ((), ())), preferred_element_type=F32,
        )
        q_s[rows_of(i, ROWS // 2), :] = rounded(out[:, 0:CH])
        k_s[rows_of(i, ROWS // 2), :] = rounded(out[:, CH:2 * CH])
        v_s[rows_of(i, ROWS // 2), :] = rounded(out[:, 2 * CH:3 * CH])
        return carry

    lax.fori_loop(0, 2, project, 0)

    def gate(i, carry):
        at = rows_of(i, POS)
        g_s[at, :] = rounded(k_s[at, :] * v_s[at, :])
        s_s[at, :] = rounded(cot_s[at, :] * q_s[at, :])
        return carry

    lax.fori_loop(0, X, gate, 0)

    def states(t, carry):
        up, down = carry
        g_now = g_s[pl.ds(t, 8, stride=SUB), :]
        s_now = s_s[pl.ds(SUB - 1 - t, 8, stride=SUB), :]
        return (
            tuple(a_t[m] * up[m] + g_now for m in range(M)),
            tuple(a_t[m] * down[m] + s_now for m in range(M)),
        )

    zero = tuple(jnp.zeros((8, CH), F32) for _ in range(M))
    up, down = lax.fori_loop(0, SUB, states, (zero, zero))
    piece = lax.broadcasted_iota(jnp.int32, (8, CH), 0)
    for m in range(M):
        lost = decay[m:m + 1, :]
        fore, aft = up[m], down[m]
        for shift in (1, 2, 4):
            keep = jnp.exp(lost * (-float(SUB * shift)))
            fore = fore + jnp.where(piece >= shift, keep * pltpu.roll(fore, shift, 0), 0.0)
            aft = aft + jnp.where(piece < 8 - shift, keep * pltpu.roll(aft, 8 - shift, 0), 0.0)
        eb[0, m:m + 1, :] = fore[7:8, :]
        eb[1, m:m + 1, :] = aft[0:1, :]
        cl_t[m] = jnp.where(piece >= 1, pltpu.roll(fore, 1, 0), 0.0)
        cb_t[m] = jnp.where(piece < 7, pltpu.roll(aft, 7, 0), 0.0)

    states_out = []
    for i in sorted(range(1, ZH), key=lambda i: (-(i % H), abs(i - ZH // 2))):
        to = lax.rem(me + i, ZH)
        which = jnp.where(to > me, 0, 1)
        states_out.append(remote(
            eb.at[which], st.at[me], st_ss.at[i], st_rs.at[i],
            {"z": lax.div(to, H), "h": lax.rem(to, H)},
        ))
    gathered = list(sends)
    sends.clear()
    launch(states_out)
    for copy in gathered:
        copy.wait_send()
    arrived(states_out)

    far_keep = jnp.exp(decay * (-float(ROWS)))
    none = jnp.zeros((M, CH), F32)
    before = lax.fori_loop(0, me, lambda j, s: far_keep * s + st[j], none)
    after = lax.fori_loop(0, ZH - 1 - me, lambda j, s: far_keep * s + st[ZH - 1 - j], none)

    place = piece.astype(F32) * float(SUB)
    start_up, start_down = [], []
    for m in range(M):
        lost = decay[m:m + 1, :]
        start_up.append(cl_t[m] + jnp.exp(-lost * place) * before[m:m + 1, :])
        start_down.append(
            cb_t[m] + jnp.exp(-lost * (float(SUB * 7) - place)) * after[m:m + 1, :]
        )

    def forward(t, carry):
        up, total = carry
        at = pl.ds(t, 8, stride=SUB)
        g_now, s_now = g_s[at, :], s_s[at, :]
        up = tuple(a_t[m] * up[m] + g_now for m in range(M))
        conv_s[at, :] = tree_sum(r_t[m] * up[m] for m in range(M))
        return up, tuple(total[m] + s_now * up[m] for m in range(M))

    def backward(t, down):
        at = pl.ds(SUB - 1 - t, 8, stride=SUB)
        s_now = s_s[at, :]
        down = tuple(a_t[m] * down[m] + s_now for m in range(M))
        back_s[at, :] = tree_sum(r_t[m] * down[m] for m in range(M))
        return down

    _, total = lax.fori_loop(0, SUB, forward, (tuple(start_up), zero))
    lax.fori_loop(0, SUB, backward, tuple(start_down))

    def gates(i, carry):
        at = rows_of(i, POS)
        conv, back = rounded(conv_s[at, :]), rounded(back_s[at, :])
        g_mat[at, 0:CH] = (cot_s[at, :] * conv).astype(BF16)
        g_mat[at, CH:2 * CH] = (back * v_s[at, :]).astype(BF16)
        g_mat[at, 2 * CH:3 * CH] = (back * k_s[at, :]).astype(BF16)
        return carry

    lax.fori_loop(0, X, gates, 0)

    def outputs(i, carry):
        at = rows_of(i, POS)
        hyena = jnp.transpose(q_s[at, :] * rounded(conv_s[at, :]))
        hy_t[i] = hyena.reshape(ZH, OWN, POS).astype(BF16)
        return carry

    def send_outputs():
        lax.fori_loop(0, X, outputs, 0)
        hyenas = launch([
            remote(
                hy_t.at[lax.rem(x + i, X)], hy_o.at[:, x], hy_ss.at[i - 1], hy_rs.at[i - 1],
                {"x": lax.rem(x + i, X)},
            )
            for i in range(1, X)
        ])
        hy_o[:, x] = hy_t[x]
        gr_s[...] = jnp.zeros_like(gr_s)
        norm = 1.0 / math.sqrt(length)
        for m in range(M):
            gr_s[m:m + 1, :] = jnp.sum(total[m], axis=0, keepdims=True) * (width[m:m + 1, :] * norm)
        gr_t[...] = jnp.transpose(gr_s[...])
        owners = []
        for i in range(1, ZH):
            to = lax.rem(me + i, ZH)
            owners.append(remote(
                gr_t.at[rows_of(to, OWN), :], gr_r.at[i], gr_ss.at[i], gr_rs.at[i],
                {"z": lax.div(to, H), "h": lax.rem(to, H)},
            ))
        return hyenas, launch(owners)

    def product(j, mine):
        parity = core if mine else 1 - core
        col = pl.multiple_of((j // PARTS * NC + parity) * COLS + j % PARTS * WIDE, WIDE)

        def tile(i, carry):
            at = rows_of(i, ROWS)
            out = jnp.dot(
                g_mat[at, :], wg[:, :, pl.ds(col, WIDE)].reshape(3 * CH, WIDE),
                preferred_element_type=F32,
            )
            if mine:
                acc[j, at, :] = out
            else:
                d_s[j, at, :] = out.astype(BF16)
            return carry

        tile(0, 0)

    def chip_sum(j, owner):
        at = rows_of(owner, POS)
        return acc[j, at, :] + d_r[j, at, :].astype(F32)

    cores, first, second, finals = {}, {}, {}, {}

    def stage_product(j):
        product(j, False)
        cores[j] = launch((remote(d_s.at[j], d_r.at[j], d_ss.at[j], d_rs.at[j], {"c": 1 - core}),))
        product(j, True)

    def stage_first(j):
        arrived(cores[j])
        other = chip_sum(j, x_far)
        m1_s[j, 0] = other[:, 0:HALF].astype(BF16)
        m1_s[j, 1] = other[:, HALF:WIDE].astype(BF16)
        first[j] = launch([
            remote(m1_s.at[j, w], m1_r.at[j, w], m1_ss.at[j, w], m1_rs.at[j, w], {"x": x_up if w == 0 else x_down})
            for w in (0, 1)
        ])

    def stage_second(j):
        arrived(first[j])
        for w in (0, 1):
            side = chip_sum(j, x_up if w == 0 else x_down)
            cut = slice(0, HALF) if w == 0 else slice(HALF, WIDE)
            rest = slice(HALF, WIDE) if w == 0 else slice(0, HALF)
            m2_s[j, w, :, cut] = (side[:, cut] + m1_r[j, w].astype(F32)).astype(BF16)
            m2_s[j, w, :, rest] = side[:, rest].astype(BF16)
        second[j] = launch([
            remote(m2_s.at[j, w], m2_r.at[j, w], m2_ss.at[j, w], m2_rs.at[j, w], {"x": x_up if w == 0 else x_down})
            for w in (0, 1)
        ])

    def stage_third(j):
        arrived(second[j])
        total_x = chip_sum(j, x) + m2_r[j, 0].astype(F32) + m2_r[j, 1].astype(F32)
        owner, part = j // PARTS, j % PARTS
        copy = remote(
            y_s.at[j], y_r.at[ell, part], y_ss.at[j], y_rs.at[ell, part], {"l": jnp.int32(owner)}
        )
        finals[j] = copy

        @pl.when(ell == owner)
        def _():
            y_own[part] = total_x

        @pl.when(ell != owner)
        def _():
            y_s[j] = total_x.astype(BF16)
            copy.start()

    for i in range(PIECES + 7):
        for late, stage in ((0, stage_product), (2, stage_first), (5, stage_second), (7, stage_third)):
            if 0 <= i - late < PIECES:
                stage(ORDER[i - late])
        if i == 1:
            hyenas, owners = send_outputs()
        if i == PIECES + 3:
            arrived(hyenas)
            hyena_out[...] = hy_o[...]
            arrived(owners)
            share = gr_t[rows_of(me, OWN), :]
            for source in range(1, ZH):
                share = share + gr_r[source]
            grad_residue[...] = share[:, 0:M]

    for j in range(NL):
        @pl.when(ell != j)
        def _():
            for part in range(PARTS):
                piece_at = j * PARTS + part
                remote(
                    y_s.at[piece_at], y_r.at[j, part], y_ss.at[piece_at], y_rs.at[j, part], {"l": jnp.int32(j)}
                ).wait_recv()
                y_own[part] += y_r[j, part].astype(F32)
                finals[piece_at].wait_send()
    for part in range(PARTS):
        grad_input[:, part * WIDE:(part + 1) * WIDE] = y_own[part].astype(BF16)
    for copy in sends:
        copy.wait_send()


def hand_over(hyena, grad, residue, hyena_out, grad_out, residue_out):
    hyena_out[...] = hyena[...]
    grad_out[...] = grad[...]
    residue_out[...] = residue[...]


def shards(tokens, weights, residues, decay_rates, cotangent, length):
    wts = jnp.transpose(weights[0], (1, 0, 2))
    cot = cotangent.reshape(ZH, X, OWN, POS)
    dma = pltpu.SemaphoreType.DMA
    scratch = [
        pltpu.VMEM((ROWS, D), BF16),
        pltpu.VMEM((3, CH, D), BF16),
        pltpu.VMEM((OWN, 128), F32),
        pltpu.VMEM((CH, 128), F32),
        pltpu.VMEM((X, ZH, OWN, POS), BF16),
    ]
    scratch += [pltpu.VMEM((ROWS, CH), F32)] * 8
    scratch += [pltpu.VMEM((M, 8, CH), F32)] * 4
    scratch += [
        pltpu.VMEM((2, M, CH), F32),
        pltpu.VMEM((ZH, M, CH), F32),
        pltpu.VMEM((CH, CH), F32),
        pltpu.VMEM((CH, CH), F32),
        pltpu.VMEM((ZH, OWN, CH), F32),
        pltpu.VMEM((X, ZH, OWN, POS), BF16),
        pltpu.VMEM((ZH, X, OWN, POS), BF16),
        pltpu.VMEM((ROWS, 3 * CH), BF16),
        pltpu.VMEM((PIECES, ROWS, WIDE), F32),
        pltpu.VMEM((PIECES, ROWS, WIDE), BF16),
        pltpu.VMEM((PIECES, ROWS, WIDE), BF16),
        pltpu.VMEM((PIECES, 2, POS, HALF), BF16),
        pltpu.VMEM((PIECES, 2, POS, HALF), BF16),
        pltpu.VMEM((PIECES, 2, POS, WIDE), BF16),
        pltpu.VMEM((PIECES, 2, POS, WIDE), BF16),
        pltpu.VMEM((PIECES, POS, WIDE), BF16),
        pltpu.VMEM((NL, PARTS, POS, WIDE), BF16),
        pltpu.VMEM((PARTS, POS, WIDE), F32),
    ]
    steps = Z // 2
    scratch += [dma((3,))]
    for shape in (
        (2, 2, steps, CHUNKS), (2, 2, steps), (CHUNKS + 1,), (2, 3), (6,), (X - 1,), (ZH,), (ZH,), (X - 1,),
        (PIECES,), (PIECES, 2), (PIECES, 2),
    ):
        scratch += [dma(shape), dma(shape)]
    scratch += [dma((PIECES,)), dma((NL, PARTS))]
    vmem, hbm = pl.BlockSpec(memory_space=pltpu.VMEM), pl.BlockSpec(memory_space=pl.ANY)
    hyena, grad, residue = pl.pallas_call(
        functools.partial(body, length),
        out_shape=(
            pltpu.VMEM((ZH, X, OWN, POS), BF16),
            pltpu.VMEM((POS, COLS), BF16),
            pltpu.VMEM((OWN, M), F32),
        ),
        in_specs=[hbm, hbm, vmem, vmem, hbm],
        out_specs=(vmem, vmem, vmem),
        scratch_shapes=scratch,
        compiler_params=pltpu.CompilerParams(
            collective_id=0, has_side_effects=True, vmem_limit_bytes=60 * 1024 * 1024
        ),
        name="hyena_block",
    )(tokens, wts, residues, decay_rates, cot)
    hyena, grad, residue = pl.pallas_call(
        hand_over,
        out_shape=(
            jax.ShapeDtypeStruct((ZH, X, OWN, POS), BF16),
            jax.ShapeDtypeStruct((POS, COLS), BF16),
            jax.ShapeDtypeStruct((OWN, M), F32),
        ),
        in_specs=[vmem, vmem, vmem],
        out_specs=(vmem, vmem, vmem),
        compiler_params=pltpu.CompilerParams(vmem_limit_bytes=4 * 1024 * 1024),
        name="results",
    )(hyena, grad, residue)
    return (hyena.reshape(X * ZH * OWN, POS), grad, residue[None])


def solution(mesh):
    fine = Mesh(mesh.devices.reshape(SIZES), AXES)
    ctx, tp = ("z", "h", "x"), ("l", "c")

    def step(tokens, weights, residues, decay_rates, cotangent):
        return jax.shard_map(
            functools.partial(shards, length=tokens.shape[0]),
            mesh=fine,
            in_specs=(P(ctx, None), P(tp, ctx), P(tp, ctx), P(tp, ctx), P(tp, ctx)),
            out_specs=(P(tp, ctx), P(ctx, tp), P(tp, ctx)),
            check_vma=False,
        )(tokens, weights, residues, decay_rates, cotangent)

    return step
```
